32 devices in a mesh: group: 1, seq: 32 (over z, y, x, core).
Axes of the slice: x: 2, y: 2, z: 4, core: 2. Of those that a mesh axis runs over, the one named last changes fastest.
Arguments:
- enc_x: bfloat16 [256, 1280], P(('group', 'seq')), may hold values from -1.5 to 1.5
- enc_qkv: bfloat16 [256, 3, 640], P(('group', 'seq'))
- w_eo: bfloat16 [640, 1280], replicated, may hold values from -0.25 to 0.25
- w_kv: bfloat16 [1280, 2048], replicated, may hold values from -0.15625 to 0.15625
- dec_x: bfloat16 [32, 8192], P(('group', 'seq')), may hold values from -1.5 to 1.5
- w_q: bfloat16 [8192, 8192], P(None, 'seq'), may hold values from -0.0625 to 0.0625
- w_o: bfloat16 [8192, 8192], P(None, 'seq'), may hold values from -0.0625 to 0.0625
- cache_kv: bfloat16 [32, 4, 128, 2048], P(('group', 'seq'))
- doc_tile: int32 [32], P(('group', 'seq')), may hold values from 0 to 1
- cached_count: int32 [32], P(('group', 'seq')), may hold values from 0 to 3
Outputs:
- dec_out: bfloat16 [32, 8192], P(('group', 'seq'))
The draws below stay inside these ranges and needn't reach their ends.
All inputs are finite; a program needn't handle non-finite values.
Results may differ from the reference program's by a relative error of at most 0.017.
The reference program's roundings to bfloat16 on the way count: a program that leaves them out, or rounds other values in their place, can miss the bound.
Values may be sent and summed in bfloat16 or wider, within the bound.
A program may use at most 64 MiB of HBM per device.

```python
import jax
import jax.numpy as jnp
from jax import lax

EW = 1280
EH = 8
EHD = 80
D = 8192
HD = 128
TILE_LEN = 128
SLOTS = 4
EA = 640
KVW = 1024
ETOK = 256
NEW_TILES = 2
DOCS = 32


def draw_enc_qkv(key, part):
    first = jax.random.fold_in(jax.random.fold_in(key, 11), 0)
    base = jax.random.normal(first, (ETOK, 3, EA), jnp.float32)
    which = jnp.arange(3).reshape(1, 3, 1) == 0
    scale = jnp.full((ETOK, 1, 1), 1.8, jnp.float32)
    base = base * jnp.where(which, scale, 1.0)
    return base.astype(jnp.bfloat16)


def draw_cache_kv(key, part):
    first = jax.random.fold_in(jax.random.fold_in(key, 23), 0)
    base = jax.random.normal(first, (DOCS, SLOTS, TILE_LEN, 2 * KVW), jnp.float32)
    return base.astype(jnp.bfloat16)


def with_ends(entries, own_key, least, top_value):
    spot = [jax.random.randint(jax.random.fold_in(own_key, axis), (), 0, length) for axis, length in enumerate(entries.shape)]
    longest = entries.shape.index(max(entries.shape))
    beside = spot[:longest] + [(spot[longest] + 1) % entries.shape[longest]] + spot[longest + 1:]
    return entries.at[tuple(spot)].set(least).at[tuple(beside)].set(top_value)


def level_of(key, dims, shards, smallest, top_value):
    loudness, own = 1.0, jax.random.fold_in(key, 6)
    for dim, parts in shards:
        heights = jnp.exp(jax.random.uniform(jax.random.fold_in(own, dim), (parts,), jnp.float32, smallest / len(shards), top_value / len(shards)))
        loudness = loudness * jnp.repeat(heights, dims[dim] // parts).reshape([-1 if axis == dim else 1 for axis in range(len(dims))])
    return loudness


def gaussian(own_key, dims, deviation, limit, cuts=(), kind=jnp.bfloat16):
    factor_of = level_of(own_key, dims, cuts, -0.22, 0.18) if cuts else 1.0
    drawn = jax.random.normal(own_key, dims, jnp.float32) * deviation * factor_of
    return jnp.minimum(jnp.maximum(drawn, -limit), limit).astype(kind)


def setup_inputs(seed: int = 0, part: int = 0) -> dict:
    seeds = jax.random.split(jax.random.key(seed), 11)
    part_keys = jax.random.split(jax.random.fold_in(seeds[10], part), 11)
    return {
        "enc_x": gaussian(part_keys[0], (ETOK, EW), 0.1, 1.5, ((0, 32),)),
        "enc_qkv": draw_enc_qkv(jax.random.fold_in(jax.random.fold_in(seeds[10], part), 71), part),
        "w_eo": gaussian(seeds[2], (EA, EW), EA ** -0.5, 0.25),
        "w_kv": gaussian(seeds[3], (EW, 2 * KVW), EW ** -0.5, 0.15625),
        "dec_x": gaussian(part_keys[4], (DOCS, D), 0.1, 1.5, ((0, 32),)),
        "w_q": gaussian(seeds[5], (D, D), D ** -0.5, 0.0625, ((1, 32),)),
        "w_o": gaussian(seeds[6], (D, D), D ** -0.5, 0.0625, ((1, 32),)),
        "cache_kv": draw_cache_kv(jax.random.fold_in(jax.random.fold_in(seeds[10], part), 71), part),
        "doc_tile": with_ends(jax.random.randint(part_keys[8], (DOCS,), 0, NEW_TILES), jax.random.fold_in(part_keys[8], 1), 0, NEW_TILES - 1).astype(jnp.int32),
        "cached_count": with_ends(jax.random.randint(part_keys[9], (DOCS,), 0, SLOTS), jax.random.fold_in(part_keys[9], 1), 0, SLOTS - 1).astype(jnp.int32),
    }


def layer_norm(values):
    center = values - lax.optimization_barrier(jnp.mean(values, axis=-1, keepdims=True))
    spread = lax.optimization_barrier(jnp.mean(center * center, axis=-1, keepdims=True))
    return center * lax.rsqrt(spread + 1e-05)

def doc_attend(query_row, doc_kv, filled):
    length = doc_kv.shape[0]
    width = doc_kv.shape[1] // 2
    kv_heads = width // HD
    query_heads = query_row.astype(jnp.float32).reshape(kv_heads, -1, HD)
    key_heads = doc_kv[:, :width].astype(jnp.float32).reshape(length, kv_heads, HD)
    value_heads = doc_kv[:, width:].astype(jnp.float32).reshape(length, kv_heads, HD)
    scores = jnp.einsum('gqd,kgd->gqk', query_heads, key_heads, precision=lax.Precision.HIGHEST) * HD ** (-0.5)
    inside = jnp.arange(length, dtype=jnp.int32) // TILE_LEN <= filled
    scores = jnp.where(inside[None, None, :], scores, -jnp.inf)
    weights = jax.nn.softmax(scores, axis=-1).astype(jnp.bfloat16).astype(jnp.float32)
    result = jnp.einsum('gqk,kgd->gqd', weights, value_heads, precision=lax.Precision.HIGHEST)
    return result.reshape(-1).astype(jnp.bfloat16)

def reference(enc_x, enc_qkv, w_eo, w_kv, dec_x, w_q, w_o, cache_kv, doc_tile, cached_count):
    query_all = enc_qkv[:, 0].reshape(ETOK, EH, EHD).transpose(1, 0, 2)
    key_all = enc_qkv[:, 1].reshape(ETOK, EH, EHD).transpose(1, 0, 2)
    value_all = enc_qkv[:, 2].reshape(ETOK, EH, EHD).transpose(1, 0, 2)

    def one_head(triple):
        query_head, key_head, value_head = triple
        scores = jnp.dot(query_head, key_head.T, preferred_element_type=jnp.float32) * EHD ** (-0.5)
        weights = jax.nn.softmax(scores, axis=-1).astype(jnp.bfloat16)
        return jnp.dot(weights, value_head, preferred_element_type=jnp.float32)
    heads_out = lax.map(one_head, (query_all, key_all, value_all))
    enc_attn = heads_out.transpose(1, 0, 2).reshape(ETOK, EA).astype(jnp.bfloat16)
    resid = enc_x.astype(jnp.float32) + jnp.dot(enc_attn, w_eo, preferred_element_type=jnp.float32)
    features = layer_norm(resid).astype(jnp.bfloat16)
    new_kv = jnp.dot(features, w_kv, preferred_element_type=jnp.float32).astype(jnp.bfloat16)
    tiles = new_kv.reshape(NEW_TILES, TILE_LEN, 2 * KVW)
    x_float = dec_x.astype(jnp.float32)
    normed = (x_float * lax.rsqrt(lax.optimization_barrier(jnp.mean(x_float * x_float, axis=-1, keepdims=True)) + 1e-05)).astype(jnp.bfloat16)
    queries = jnp.dot(normed, w_q, preferred_element_type=jnp.float32).astype(jnp.bfloat16)

    def one_doc(quad):
        query_row, cache_doc, tile_id, filled = quad
        chosen = lax.dynamic_index_in_dim(tiles, tile_id.astype(jnp.int32), 0, keepdims=True)
        zero = jnp.zeros((), jnp.int32)
        doc_kv = lax.dynamic_update_slice(cache_doc, chosen, (filled.astype(jnp.int32), zero, zero))
        return doc_attend(query_row, doc_kv.reshape(SLOTS * TILE_LEN, 2 * KVW), filled)
    dec_attn = lax.map(one_doc, (queries, cache_kv, doc_tile, cached_count))
    attn_out = jnp.dot(dec_attn, w_o, preferred_element_type=jnp.float32).astype(jnp.bfloat16)
    return (x_float + attn_out.astype(jnp.float32)).astype(jnp.bfloat16)
```

```python
import functools

import jax
import jax.numpy as jnp
from jax import lax
from jax.experimental import pallas as pl
from jax.experimental.pallas import tpu as pltpu
from jax.sharding import PartitionSpec as P

EH = 8
EHD = 80
HD = 128
TILE_LEN = 128
MESH = pl.DeviceIdType.MESH


def layer_norm(values):
    center = values - jnp.mean(values, axis=-1, keepdims=True)
    spread = jnp.mean(center * center, axis=-1, keepdims=True)
    return center * lax.rsqrt(spread + 1e-05)


def doc_attend(query_row, doc_kv, filled):
    length = doc_kv.shape[0]
    width = doc_kv.shape[1] // 2
    kv_heads = width // HD
    query_heads = query_row.reshape(kv_heads, -1, HD)
    key_heads = doc_kv[:, :width].reshape(length, kv_heads, HD)
    value_heads = doc_kv[:, width:].reshape(length, kv_heads, HD)
    scores = jnp.einsum(
        "gqd,kgd->gqk", query_heads, key_heads, preferred_element_type=jnp.float32
    ) * HD ** (-0.5)
    inside = jnp.arange(length, dtype=jnp.int32) // TILE_LEN <= filled
    scores = jnp.where(inside[None, None, :], scores, -jnp.inf)
    weights = jax.nn.softmax(scores, axis=-1).astype(jnp.bfloat16)
    result = jnp.einsum("gqk,kgd->gqd", weights, value_heads, preferred_element_type=jnp.float32)
    return result.reshape(1, -1).astype(jnp.bfloat16)


def local(enc_x, enc_qkv, w_eo, w_kv, dec_x, w_q, w_o, cache_kv, doc_tile, cached_count):
    tok_rows = enc_x.shape[0]
    query_heads = enc_qkv[:, 0].reshape(tok_rows, EH, EHD)
    key_piece = lax.all_gather(enc_qkv[:, 1], "seq", axis=0, tiled=True)
    value_piece = lax.all_gather(enc_qkv[:, 2], "seq", axis=0, tiled=True)
    length = key_piece.shape[0]
    key_heads = key_piece.reshape(length, EH, EHD)
    value_heads = value_piece.reshape(length, EH, EHD)
    scores = jnp.einsum(
        "qhd,khd->hqk", query_heads, key_heads, preferred_element_type=jnp.float32
    ) * EHD ** (-0.5)
    old_max = jnp.full((EH, tok_rows), -1e30, jnp.float32)
    new_max = jnp.maximum(old_max, jnp.max(scores, axis=-1))
    powers = jnp.exp(scores - new_max[:, :, None])
    new_total = jnp.sum(powers, axis=-1)
    new_acc = jnp.einsum(
        "hqk,khd->hqd", powers.astype(jnp.bfloat16), value_heads, preferred_element_type=jnp.float32
    )
    enc_attn = (
        (new_acc / new_total[:, :, None])
        .transpose(1, 0, 2)
        .reshape(tok_rows, -1)
        .astype(jnp.bfloat16)
    )
    resid = enc_x.astype(jnp.float32) + jnp.dot(enc_attn, w_eo, preferred_element_type=jnp.float32)
    features = layer_norm(resid).astype(jnp.bfloat16)
    tile_start = doc_tile[0] * TILE_LEN
    x_float = dec_x.astype(jnp.float32)
    normed = (
        x_float * lax.rsqrt(jnp.mean(x_float * x_float, axis=-1, keepdims=True) + 1e-05)
    ).astype(jnp.bfloat16)
    query_cols = jnp.dot(
        lax.all_gather(normed, "seq", axis=0, tiled=True), w_q, preferred_element_type=jnp.float32
    ).astype(jnp.bfloat16)
    query_row = lax.all_to_all(query_cols, "seq", split_axis=0, concat_axis=1, tiled=True)
    zero = jnp.zeros((), jnp.int32)
    filled = cached_count[0]
    local_kv = jnp.dot(features, w_kv, preferred_element_type=jnp.float32).astype(jnp.bfloat16)
    buffer = jnp.zeros((TILE_LEN, w_kv.shape[1]), jnp.bfloat16)
    piece = lax.all_gather(local_kv, "seq", axis=0, tiled=True)
    length = piece.shape[0]
    position = jnp.arange(length, dtype=jnp.int32) - tile_start
    inside = (position >= 0) & (position < buffer.shape[0])
    clipped = jnp.clip(position, 0, buffer.shape[0] - 1)
    tile_kv = buffer.at[clipped].add(jnp.where(inside[:, None], piece, jnp.zeros_like(piece)))
    doc_kv = lax.dynamic_update_slice(cache_kv[0], tile_kv[None], (filled, zero, zero))
    doc_kv = doc_kv.reshape(-1, doc_kv.shape[-1])
    dec_attn = doc_attend(query_row[0], doc_kv, filled)
    output_cols = jnp.dot(
        lax.all_gather(dec_attn, "seq", axis=0, tiled=True), w_o, preferred_element_type=jnp.float32
    ).astype(jnp.bfloat16)
    attn_out = lax.all_to_all(output_cols, "seq", split_axis=0, concat_axis=1, tiled=True)
    return (x_float + attn_out.astype(jnp.float32)).astype(jnp.bfloat16)


def fused_kernel(
    n, qkv_hbm, resid_hbm, x_hbm, tile_ref, count_ref, weo_hbm, wkv_hbm, wq_hbm, wo_hbm, cache_hbm, out_ref,
    weo, wkv, wq, wo, cache, load_sem, x_own,
    enc_own, enc_all, enc_send, enc_recv, enc_rows, enc_feat, new_kv,
    x_rows, norm_own, norm_all, norm_send, norm_recv,
    attn_heads, attn_own, attn_all, attn_send, attn_recv,
    wide, lhs, head_rows, old_scores,
    q_out, q_in, q_send, q_recv,
    o_out, o_in, o_send, o_recv,
):
    me = lax.axis_index("seq")
    inner = 4
    outer = n // (2 * inner)
    zi, qi, ci = me // (2 * inner), (me // 2) % inner, me % 2

    def at(kz, kq, kc):
        return (zi + kz) % outer * (2 * inner) + (qi + kq) % inner * 2 + (ci + kc) % 2

    barrier = pltpu.get_barrier_semaphore()

    partners = [at(kz, 0, 0) for kz in range(1, outer)] + [at(0, kq, 0) for kq in range(1, inner)] + [at(0, 0, 1)]
    for partner in partners:
        pl.semaphore_signal(barrier, inc=1, device_id={"seq": partner}, device_id_type=MESH)

    wide_a = EH * EHD
    small = [
        pltpu.make_async_copy(src, dst, load_sem.at[5 + i])
        for i, (src, dst) in enumerate(
            [(x_hbm, x_own)]
            + [(qkv_hbm.at[j], enc_own.at[:, pl.ds(j * wide_a, wide_a)]) for j in range(3)]
            + [(resid_hbm, enc_own.at[:, pl.ds(3 * wide_a, resid_hbm.shape[1])])]
        )
    ]
    for load in small:
        load.start()
    loads = [
        pltpu.make_async_copy(src, dst, load_sem.at[i])
        for i, (src, dst) in enumerate(
            ((wq_hbm, wq), (weo_hbm, weo), (wkv_hbm, wkv), (cache_hbm, cache), (wo_hbm, wo))
        )
    ]
    for load in loads:
        load.start()

    small[0].wait()
    heads = x_rows.shape[0]
    for k in range(heads):
        x_rows[k:k + 1, :] = x_own[:, k * HD:(k + 1) * HD].astype(jnp.float32)
    x_float = x_rows[...]
    squares = jnp.sum(jnp.sum(x_float * x_float, axis=1, keepdims=True), axis=0, keepdims=True)
    normed = (x_float * lax.rsqrt(squares / x_float.size + 1e-05)).astype(jnp.bfloat16)
    norm_own[...] = normed
    norm_all[me] = normed
    for load in small[1:]:
        load.wait()
    enc_all[me] = enc_own[...]
    pl.semaphore_wait(barrier, len(partners))

    flip_x = qi + 1 - 2 * (qi % 2)
    flip_y = (qi + 2) % inner
    flip_both = (flip_x + 2) % inner

    def place(kz, plane, core):
        return (zi + kz + outer) % outer * (2 * inner) + plane * 2 + core

    def gather(own, every, send, recv, relay):
        near, side, far, core = 0, (outer - 1, 2 * outer - 1), 3 * outer - 1, 4 * outer - 1

        def copy(src, slot, mark, device):
            return pltpu.make_async_remote_copy(
                src_ref=src, dst_ref=every.at[slot], send_sem=send.at[0], recv_sem=recv.at[mark],
                device_id={"seq": device}, device_id_type=MESH,
            )

        def push(src, slot, mark, device):
            copy(src, slot, mark, device).start()

        def take(slot, mark):
            copy(own, slot, mark, place(0, qi, 1 - ci)).wait_recv()

        def spread(src, slot, kz):
            if not relay:
                push(src, slot, far + kz, place(0, flip_both, ci))
            push(src, slot, side[0] + kz, place(0, flip_x, ci))
            push(src, slot, side[1] + kz, place(0, flip_y, ci))
            push(src, slot, core, place(0, qi, 1 - ci))

        def first():
            for kz in range(1, outer):
                push(own, me, near + kz - 1, place(kz, qi, ci))
            spread(own, me, 0)

        def second():
            for kz in range(1, outer):
                slot = place(-kz, qi, ci)
                take(slot, near + kz - 1)
                spread(every.at[slot], slot, kz)

        def third():
            for kz in range(outer):
                for odd, (plane, onward) in enumerate(((flip_x, flip_y), (flip_y, flip_x))):
                    slot = place(-kz, plane, ci)
                    take(slot, side[odd] + kz)
                    if relay and kz % 2 == odd:
                        push(every.at[slot], slot, far + kz, place(0, onward, ci))
                    push(every.at[slot], slot, core, place(0, qi, 1 - ci))

        def fourth():
            for kz in range(outer):
                slot = place(-kz, flip_both, ci)
                take(slot, far + kz)
                push(every.at[slot], slot, core, place(0, qi, 1 - ci))

        def last():
            half = every.at[pl.ds(0, n // 2)]
            copy(half, pl.ds(0, n // 2), core, place(0, qi, 1 - ci)).wait_recv()

        def drain():
            most = every.at[pl.ds(0, n - 1)]
            copy(most, pl.ds(0, n - 1), core, place(0, qi, 1 - ci)).wait_send()

        return first, second, third, fourth, last, drain

    def scatter(values, out, into, send, recv):
        rounded = values.astype(jnp.bfloat16).astype(jnp.float32)
        for d in range(n):
            for half in range(2):
                out[d, half:half + 1, :] = rounded[d:d + 1, half * HD:(half + 1) * HD]

        def one(k, carry):
            device = (me + k) % n
            pltpu.make_async_remote_copy(
                src_ref=out.at[device], dst_ref=into.at[me], send_sem=send.at[0], recv_sem=recv.at[0],
                device_id={"seq": device}, device_id_type=MESH,
            ).start()
            return carry

        lax.fori_loop(1, n, one, 0)
        into[me] = out[me]

    def collect(out, into, send, recv):
        copy = pltpu.make_async_remote_copy(
            src_ref=out.at[pl.ds(0, n - 1)], dst_ref=into.at[pl.ds(0, n - 1)], send_sem=send.at[0], recv_sem=recv.at[0],
            device_id={"seq": place(0, qi, 1 - ci)}, device_id_type=MESH,
        )
        copy.wait_recv()
        copy.wait_send()
        for d in range(n):
            head_rows[2 * d:2 * d + 2, :] = into[d]

    def project(every, weight):
        wide[...] = every[...].astype(jnp.float32).reshape(n * heads, HD)
        for k in range(heads):
            lhs[:, k * HD:(k + 1) * HD] = wide[pl.ds(k, n, stride=heads), :].astype(jnp.bfloat16)
        return jnp.dot(lhs[...], weight[...], preferred_element_type=jnp.float32)

    norm_first, norm_second, norm_third, norm_fourth, norm_last, norm_drain = gather(
        norm_own, norm_all, norm_send, norm_recv, False
    )
    enc_first, enc_second, enc_third, enc_fourth, enc_last, enc_drain = gather(
        enc_own, enc_all, enc_send, enc_recv, True
    )
    norm_first()
    enc_first()
    norm_second()
    enc_second()
    norm_third()
    norm_fourth()
    norm_last()
    loads[0].wait()
    scatter(project(norm_all, wq), q_out, q_in, q_send, q_recv)
    enc_third()
    enc_fourth()
    loads[3].wait()
    collect(q_out, q_in, q_send, q_recv)
    width = new_kv.shape[1] // 2
    kv_heads = width // HD
    each = heads // kv_heads
    flip = (((1,), (1,)), ((), ()))
    for g in range(kv_heads):
        old_scores[g * each:(g + 1) * each, :] = lax.dot_general(
            head_rows[g * each:(g + 1) * each, :].astype(jnp.bfloat16),
            cache[:, :, g * HD:(g + 1) * HD].reshape(-1, HD), flip, preferred_element_type=jnp.float32,
        ) * HD ** (-0.5)
    enc_last()

    tok_rows = enc_own.shape[0]
    group = 32 // tok_rows

    def unpack(j, carry):
        block = enc_all[pl.ds(j * group, group), :, wide_a:3 * wide_a].astype(jnp.float32)
        enc_rows[pl.ds(pl.multiple_of(j * 32, 32), 32), :] = block.reshape(32, -1).astype(jnp.bfloat16)
        return carry

    lax.fori_loop(0, n // group, unpack, 0)
    each_tile = TILE_LEN // tok_rows

    def own_tile(cols):
        rows = None
        for t in range(n // each_tile):
            there = enc_all[t * each_tile:(t + 1) * each_tile, :, cols].astype(jnp.float32)
            there = there.reshape(TILE_LEN, -1)
            if rows is None:
                rows, chosen = there, jnp.broadcast_to(tile_ref[...], there.shape)
            else:
                rows = jnp.where(chosen == t, there, rows)
        return rows

    queries = own_tile(slice(0, wide_a)).astype(jnp.bfloat16)
    columns = [None] * (wide_a // HD)
    for h in range(EH):
        low, high = h * EHD // HD, (h * EHD + EHD - 1) // HD + 1
        span = slice(low * HD, high * HD)
        lane = lax.broadcasted_iota(jnp.int32, (TILE_LEN, (high - low) * HD), 1) + low * HD
        inside = (lane >= h * EHD) & (lane < (h + 1) * EHD)
        picked = jnp.where(inside, queries[:, span], jnp.zeros_like(queries[:, span]))
        scores = lax.dot_general(
            picked, enc_rows[:, span], (((1,), (1,)), ((), ())), preferred_element_type=jnp.float32
        ) * EHD ** (-0.5)
        powers = jnp.exp(scores - jnp.max(scores, axis=-1, keepdims=True))
        weights = (powers / jnp.sum(powers, axis=-1, keepdims=True)).astype(jnp.bfloat16)
        part = jnp.dot(
            weights, enc_rows[:, wide_a + low * HD:wide_a + high * HD], preferred_element_type=jnp.float32
        )
        for b in range(low, high):
            here = slice((b - low) * HD, (b - low + 1) * HD)
            columns[b] = part[:, here] if columns[b] is None else jnp.where(inside[:, here], part[:, here], columns[b])
    enc_attn = jnp.concatenate(columns, axis=1).astype(jnp.bfloat16)
    loads[1].wait()
    resid = own_tile(slice(3 * wide_a, enc_own.shape[1])) + jnp.dot(
        enc_attn, weo[...], preferred_element_type=jnp.float32
    )
    enc_feat[...] = layer_norm(resid).astype(jnp.bfloat16)
    loads[2].wait()

    def kv_columns(j, carry):
        cols = pl.ds(pl.multiple_of(j * 512, 512), 512)
        new_kv[:, cols] = jnp.dot(
            enc_feat[...], wkv[:, cols], preferred_element_type=jnp.float32
        ).astype(jnp.bfloat16)
        return carry

    lax.fori_loop(0, new_kv.shape[1] // 512, kv_columns, 0)

    slots = cache.shape[0]
    token = lax.broadcasted_iota(jnp.int32, (each, slots * TILE_LEN), 1)
    cached = token // TILE_LEN < jnp.broadcast_to(count_ref[...], token.shape)
    for g in range(kv_heads):
        query = head_rows[g * each:(g + 1) * each, :].astype(jnp.bfloat16)
        keys = slice(g * HD, (g + 1) * HD)
        values = slice(width + g * HD, width + (g + 1) * HD)
        old = jnp.where(cached, old_scores[g * each:(g + 1) * each, :], -jnp.inf)
        new = lax.dot_general(
            query, new_kv[:, keys], flip, preferred_element_type=jnp.float32
        ) * HD ** (-0.5)
        top = jnp.maximum(jnp.max(old, axis=-1, keepdims=True), jnp.max(new, axis=-1, keepdims=True))
        old = jnp.exp(old - top)
        new = jnp.exp(new - top)
        total = jnp.sum(old, axis=-1, keepdims=True) + jnp.sum(new, axis=-1, keepdims=True)
        attn_heads[g * each:(g + 1) * each, :] = jnp.dot(
            (old / total).astype(jnp.bfloat16), cache[:, :, values].reshape(-1, HD),
            preferred_element_type=jnp.float32,
        ) + jnp.dot(
            (new / total).astype(jnp.bfloat16), new_kv[:, values], preferred_element_type=jnp.float32
        )
    dec_attn = attn_heads[...].astype(jnp.bfloat16)
    attn_own[...] = dec_attn
    attn_all[me] = dec_attn
    attn_first, attn_second, attn_third, attn_fourth, attn_last, attn_drain = gather(
        attn_own, attn_all, attn_send, attn_recv, False
    )
    attn_first()
    attn_second()
    attn_third()
    attn_fourth()
    attn_last()
    loads[4].wait()
    scatter(project(attn_all, wo), o_out, o_in, o_send, o_recv)
    norm_drain()
    enc_drain()
    attn_drain()
    collect(o_out, o_in, o_send, o_recv)
    out_ref[...] = (x_rows[...] + head_rows[...]).astype(jnp.bfloat16)


def fused(n, enc_x, enc_qkv, w_eo, w_kv, dec_x, w_q, w_o, cache_kv, doc_tile, cached_count):
    tok_rows = enc_x.shape[0]
    packed = (tok_rows, enc_qkv.shape[1] * enc_qkv.shape[2] + enc_x.shape[1])
    heads = dec_x.shape[1] // HD
    tokens = n * tok_rows
    bf16, f32 = jnp.bfloat16, jnp.float32
    vmem = pl.BlockSpec(memory_space=pltpu.VMEM)
    hbm = pl.BlockSpec(memory_space=pl.ANY)
    dma = pltpu.SemaphoreType.DMA
    marks = n // 2
    piece = [pltpu.VMEM((heads, HD), bf16), pltpu.VMEM((n, heads, HD), bf16), dma((1,)), dma((marks,))]
    trade = [pltpu.VMEM((n, 2, HD), f32), pltpu.VMEM((n, 2, HD), f32), dma((1,)), dma((1,))]
    out = pl.pallas_call(
        functools.partial(fused_kernel, n),
        out_shape=jax.ShapeDtypeStruct((heads, HD), bf16),
        in_specs=[hbm, hbm, hbm, vmem, vmem, hbm, hbm, hbm, hbm, hbm],
        out_specs=vmem,
        scratch_shapes=[
            pltpu.VMEM(w_eo.shape, bf16),
            pltpu.VMEM(w_kv.shape, bf16),
            pltpu.VMEM(w_q.shape, bf16),
            pltpu.VMEM(w_o.shape, bf16),
            pltpu.VMEM(cache_kv.shape[1:], bf16),
            dma((10,)),
            pltpu.VMEM(dec_x.shape, bf16),
            pltpu.VMEM(packed, bf16),
            pltpu.VMEM((n,) + packed, bf16),
            dma((1,)),
            dma((marks,)),
            pltpu.VMEM((tokens, 2 * enc_qkv.shape[2]), bf16),
            pltpu.VMEM((TILE_LEN, enc_x.shape[1]), bf16),
            pltpu.VMEM((TILE_LEN, w_kv.shape[1]), bf16),
            pltpu.VMEM((heads, HD), f32),
            *piece,
            pltpu.VMEM((heads, HD), f32),
            *piece,
            pltpu.VMEM((n * heads, HD), f32),
            pltpu.VMEM((n, heads * HD), bf16),
            pltpu.VMEM((heads, HD), f32),
            pltpu.VMEM((heads, cache_kv.shape[1] * TILE_LEN), f32),
            *trade,
            *trade,
        ],
        compiler_params=pltpu.CompilerParams(collective_id=0, has_side_effects=True),
    )(enc_qkv.transpose(1, 0, 2), enc_x, dec_x, doc_tile.reshape(1, 1), cached_count.reshape(1, 1), w_eo, w_kv, w_q, w_o, cache_kv[0])
    return out.reshape(1, -1)


def solution(mesh):
    n = mesh.shape["seq"]
    return jax.shard_map(
        functools.partial(fused, n) if n == 32 else local,
        mesh=mesh,
        in_specs=(
            P(("group", "seq"), None),
            P(("group", "seq"), None, None),
            P(),
            P(),
            P(("group", "seq"), None),
            P(None, "seq"),
            P(None, "seq"),
            P(("group", "seq"), None, None, None),
            P(("group", "seq")),
            P(("group", "seq")),
        ),
        out_specs=P(("group", "seq"), None),
        check_vma=False,
    )
```

```python
import functools

import jax
import jax.numpy as jnp
from jax import lax
from jax.experimental import pallas as pl
from jax.experimental.pallas import tpu as pltpu
from jax.sharding import PartitionSpec as P

EH = 8
EHD = 80
HD = 128
TILE_LEN = 128
MESH = pl.DeviceIdType.MESH
LOG2E = 1.4426950408889634


def layer_norm(values):
    center = values - jnp.mean(values, axis=-1, keepdims=True)
    spread = jnp.mean(center * center, axis=-1, keepdims=True)
    return center * lax.rsqrt(spread + 1e-05)


def doc_attend(query_row, doc_kv, filled):
    length = doc_kv.shape[0]
    width = doc_kv.shape[1] // 2
    kv_heads = width // HD
    query_heads = query_row.reshape(kv_heads, -1, HD)
    key_heads = doc_kv[:, :width].reshape(length, kv_heads, HD)
    value_heads = doc_kv[:, width:].reshape(length, kv_heads, HD)
    scores = jnp.einsum(
        "gqd,kgd->gqk", query_heads, key_heads, preferred_element_type=jnp.float32
    ) * HD ** (-0.5)
    inside = jnp.arange(length, dtype=jnp.int32) // TILE_LEN <= filled
    scores = jnp.where(inside[None, None, :], scores, -jnp.inf)
    weights = jax.nn.softmax(scores, axis=-1).astype(jnp.bfloat16)
    result = jnp.einsum("gqk,kgd->gqd", weights, value_heads, preferred_element_type=jnp.float32)
    return result.reshape(1, -1).astype(jnp.bfloat16)


def local(enc_x, enc_qkv, w_eo, w_kv, dec_x, w_q, w_o, cache_kv, doc_tile, cached_count):
    tok_rows = enc_x.shape[0]
    query_heads = enc_qkv[:, 0].reshape(tok_rows, EH, EHD)
    key_piece = lax.all_gather(enc_qkv[:, 1], "seq", axis=0, tiled=True)
    value_piece = lax.all_gather(enc_qkv[:, 2], "seq", axis=0, tiled=True)
    length = key_piece.shape[0]
    key_heads = key_piece.reshape(length, EH, EHD)
    value_heads = value_piece.reshape(length, EH, EHD)
    scores = jnp.einsum(
        "qhd,khd->hqk", query_heads, key_heads, preferred_element_type=jnp.float32
    ) * EHD ** (-0.5)
    old_max = jnp.full((EH, tok_rows), -1e30, jnp.float32)
    new_max = jnp.maximum(old_max, jnp.max(scores, axis=-1))
    powers = jnp.exp(scores - new_max[:, :, None])
    new_total = jnp.sum(powers, axis=-1)
    new_acc = jnp.einsum(
        "hqk,khd->hqd", powers.astype(jnp.bfloat16), value_heads, preferred_element_type=jnp.float32
    )
    enc_attn = (
        (new_acc / new_total[:, :, None])
        .transpose(1, 0, 2)
        .reshape(tok_rows, -1)
        .astype(jnp.bfloat16)
    )
    resid = enc_x.astype(jnp.float32) + jnp.dot(enc_attn, w_eo, preferred_element_type=jnp.float32)
    features = layer_norm(resid).astype(jnp.bfloat16)
    tile_start = doc_tile[0] * TILE_LEN
    x_float = dec_x.astype(jnp.float32)
    normed = (
        x_float * lax.rsqrt(jnp.mean(x_float * x_float, axis=-1, keepdims=True) + 1e-05)
    ).astype(jnp.bfloat16)
    query_cols = jnp.dot(
        lax.all_gather(normed, "seq", axis=0, tiled=True), w_q, preferred_element_type=jnp.float32
    ).astype(jnp.bfloat16)
    query_row = lax.all_to_all(query_cols, "seq", split_axis=0, concat_axis=1, tiled=True)
    zero = jnp.zeros((), jnp.int32)
    filled = cached_count[0]
    local_kv = jnp.dot(features, w_kv, preferred_element_type=jnp.float32).astype(jnp.bfloat16)
    buffer = jnp.zeros((TILE_LEN, w_kv.shape[1]), jnp.bfloat16)
    piece = lax.all_gather(local_kv, "seq", axis=0, tiled=True)
    length = piece.shape[0]
    position = jnp.arange(length, dtype=jnp.int32) - tile_start
    inside = (position >= 0) & (position < buffer.shape[0])
    clipped = jnp.clip(position, 0, buffer.shape[0] - 1)
    tile_kv = buffer.at[clipped].add(jnp.where(inside[:, None], piece, jnp.zeros_like(piece)))
    doc_kv = lax.dynamic_update_slice(cache_kv[0], tile_kv[None], (filled, zero, zero))
    doc_kv = doc_kv.reshape(-1, doc_kv.shape[-1])
    dec_attn = doc_attend(query_row[0], doc_kv, filled)
    output_cols = jnp.dot(
        lax.all_gather(dec_attn, "seq", axis=0, tiled=True), w_o, preferred_element_type=jnp.float32
    ).astype(jnp.bfloat16)
    attn_out = lax.all_to_all(output_cols, "seq", split_axis=0, concat_axis=1, tiled=True)
    return (x_float + attn_out.astype(jnp.float32)).astype(jnp.bfloat16)


def fused_kernel(
    n, qkv_hbm, resid_hbm, x_hbm, tile_hbm, count_hbm, weo_hbm, wkv_hbm, wq_hbm, wo_hbm, cache_hbm, out_ref,
    weo, wkv, wq, wo, cache, load_sem, x_own, tile_own, count_own,
    enc_own, enc_all, enc_send, enc_recv, enc_rows, new_kv,
    x_rows, norm_own, norm_all, norm_send, norm_recv,
    attn_own, attn_all, attn_send, attn_recv,
    wide, head_rows,
    q_out, q_in, q_send, q_recv,
    o_out, o_in, o_send, o_recv,
):
    me = lax.axis_index("seq")
    inner = 4
    outer = n // (2 * inner)
    zi, qi, ci = me // (2 * inner), (me // 2) % inner, me % 2

    def at(kz, kq, kc):
        return (zi + kz) % outer * (2 * inner) + (qi + kq) % inner * 2 + (ci + kc) % 2

    barrier = pltpu.get_barrier_semaphore()

    partners = [at(kz, 0, 0) for kz in range(1, outer)] + [at(0, kq, 0) for kq in range(1, inner)] + [at(0, 0, 1)]
    for partner in partners:
        pl.semaphore_signal(barrier, inc=1, device_id={"seq": partner}, device_id_type=MESH)

    wide_a = EH * EHD
    heads = x_rows.shape[0]
    pitch = wide.shape[0] // n

    def widen(every, slot):
        wide[pl.ds(pl.multiple_of(slot * pitch, 8), heads), :] = every[slot].astype(jnp.float32)

    small = [
        pltpu.make_async_copy(src, dst, load_sem.at[5 + i])
        for i, (src, dst) in enumerate(
            [(x_hbm, x_own)]
            + [(qkv_hbm.at[j], enc_own.at[:, pl.ds(j * wide_a, wide_a)]) for j in range(3)]
            + [(resid_hbm, enc_own.at[:, pl.ds(3 * wide_a, resid_hbm.shape[1])])]
            + [(tile_hbm, tile_own), (count_hbm, count_own)]
        )
    ]
    for load in small:
        load.start()
    loads = [
        pltpu.make_async_copy(src, dst, load_sem.at[i])
        for i, (src, dst) in enumerate(
            ((wq_hbm, wq), (weo_hbm, weo), (wkv_hbm, wkv), (cache_hbm, cache), (wo_hbm, wo))
        )
    ]
    for load in loads:
        load.start()

    small[0].wait()
    for k in range(heads):
        x_rows[k:k + 1, :] = x_own[:, k * HD:(k + 1) * HD].astype(jnp.float32)
    x_float = x_rows[...]
    squares = jnp.sum(jnp.sum(x_float * x_float, axis=1, keepdims=True), axis=0, keepdims=True)
    normed = (x_float * lax.rsqrt(squares / x_float.size + 1e-05)).astype(jnp.bfloat16)
    norm_own[...] = normed
    norm_all[me] = normed
    widen(norm_all, me)
    for load in small[1:-2]:
        load.wait()
    enc_all[me] = enc_own[...]
    pl.semaphore_wait(barrier, len(partners))

    flip_x = qi + 1 - 2 * (qi % 2)
    flip_y = (qi + 2) % inner
    flip_both = (flip_x + 2) % inner

    def place(kz, plane, core):
        return (zi + kz + outer) % outer * (2 * inner) + plane * 2 + core

    def gather(own, every, send, recv, relay, ready):
        near, side, far, core = 0, (outer - 1, 2 * outer - 1), 3 * outer - 1, 4 * outer - 1

        def copy(src, slot, mark, device):
            return pltpu.make_async_remote_copy(
                src_ref=src, dst_ref=every.at[slot], send_sem=send.at[0], recv_sem=recv.at[mark],
                device_id={"seq": device}, device_id_type=MESH,
            )

        def push(src, slot, mark, device):
            copy(src, slot, mark, device).start()

        def take(slot, mark):
            copy(own, slot, mark, place(0, qi, 1 - ci)).wait_recv()

        def spread(src, slot, kz):
            if not relay:
                push(src, slot, far + kz, place(0, flip_both, ci))
            push(src, slot, side[0] + kz, place(0, flip_x, ci))
            push(src, slot, side[1] + kz, place(0, flip_y, ci))
            push(src, slot, core, place(0, qi, 1 - ci))

        def first():
            for kz in range(1, outer):
                push(own, me, near + kz - 1, place(kz, qi, ci))
            spread(own, me, 0)

        def second():
            for kz in range(1, outer):
                slot = place(-kz, qi, ci)
                take(slot, near + kz - 1)
                spread(every.at[slot], slot, kz)
                ready(every, slot)

        def third():
            for kz in range(outer):
                for odd, (plane, onward) in enumerate(((flip_x, flip_y), (flip_y, flip_x))):
                    slot = place(-kz, plane, ci)
                    take(slot, side[odd] + kz)
                    if relay and kz % 2 == odd:
                        push(every.at[slot], slot, far + kz, place(0, onward, ci))
                    push(every.at[slot], slot, core, place(0, qi, 1 - ci))
                    ready(every, slot)

        def fourth():
            for kz in range(outer):
                slot = place(-kz, flip_both, ci)
                take(slot, far + kz)
                push(every.at[slot], slot, core, place(0, qi, 1 - ci))
                ready(every, slot)

        def last():
            half = every.at[pl.ds(0, n // 2)]
            copy(half, pl.ds(0, n // 2), core, place(0, qi, 1 - ci)).wait_recv()
            for pair in range(n // 2):
                ready(every, 2 * pair + 1 - ci)

        def drain():
            most = every.at[pl.ds(0, n - 1)]
            copy(most, pl.ds(0, n - 1), core, place(0, qi, 1 - ci)).wait_send()

        return first, second, third, fourth, last, drain

    def scatter(values, out, into, send, recv):
        rounded = values.astype(jnp.bfloat16).astype(jnp.float32)
        for d in range(n):
            for half in range(2):
                out[d, half:half + 1, :] = rounded[d:d + 1, half * HD:(half + 1) * HD]

        def one(k, carry):
            device = (me + k) % n
            pltpu.make_async_remote_copy(
                src_ref=out.at[device], dst_ref=into.at[me], send_sem=send.at[0], recv_sem=recv.at[0],
                device_id={"seq": device}, device_id_type=MESH,
            ).start()
            return carry

        lax.fori_loop(1, n, one, 0)
        into[me] = out[me]

    def collect(out, into, send, recv):
        copy = pltpu.make_async_remote_copy(
            src_ref=out.at[pl.ds(0, n - 1)], dst_ref=into.at[pl.ds(0, n - 1)], send_sem=send.at[0], recv_sem=recv.at[0],
            device_id={"seq": place(0, qi, 1 - ci)}, device_id_type=MESH,
        )
        copy.wait_recv()
        copy.wait_send()
        for d in range(n):
            head_rows[2 * d:2 * d + 2, :] = into[d]

    def project(weight):
        total = None
        for k in range(0, heads, 2):
            pair = [wide[pl.ds(k + j, n, stride=pitch), :] for j in range(2)]
            term = jnp.dot(
                jnp.concatenate(pair, axis=1).astype(jnp.bfloat16), weight[k * HD:(k + 2) * HD, :],
                preferred_element_type=jnp.float32,
            )
            total = term if total is None else total + term
        return total

    norm_first, norm_second, norm_third, norm_fourth, norm_last, norm_drain = gather(
        norm_own, norm_all, norm_send, norm_recv, False, widen
    )
    enc_first, enc_second, enc_third, enc_fourth, enc_last, enc_drain = gather(
        enc_own, enc_all, enc_send, enc_recv, True, lambda every, slot: None
    )
    norm_first()
    enc_first()
    norm_second()
    enc_second()
    norm_third()
    norm_fourth()
    norm_last()
    loads[0].wait()
    scatter(project(wq), q_out, q_in, q_send, q_recv)
    enc_third()
    enc_fourth()
    loads[3].wait()
    collect(q_out, q_in, q_send, q_recv)
    width = new_kv.shape[1] // 2
    kv_heads = width // HD
    each = heads // kv_heads
    flip = (((1,), (1,)), ((), ()))
    scale = HD ** (-0.5) * LOG2E
    query = head_rows[...].astype(jnp.bfloat16)
    old = jnp.concatenate(
        [
            lax.dot_general(
                query[g * each:(g + 1) * each, :], cache[:, :, g * HD:(g + 1) * HD].reshape(-1, HD),
                flip, preferred_element_type=jnp.float32,
            )
            for g in range(kv_heads)
        ],
        axis=0,
    ) * scale
    for load in small[-2:]:
        load.wait()
    token = lax.broadcasted_iota(jnp.int32, old.shape, 1)
    cached = token // TILE_LEN < jnp.broadcast_to(count_own[0], token.shape)
    old = jnp.where(cached, old, -jnp.inf)
    old_top = jnp.max(old, axis=-1, keepdims=True)
    old = jnp.where(cached, jnp.exp2(old - old_top), 0.0)
    old_total = jnp.sum(old, axis=-1, keepdims=True)
    old = old.astype(jnp.bfloat16)
    old_attn = jnp.concatenate(
        [
            jnp.dot(
                old[g * each:(g + 1) * each, :], cache[:, :, width + g * HD:width + (g + 1) * HD].reshape(-1, HD),
                preferred_element_type=jnp.float32,
            )
            for g in range(kv_heads)
        ],
        axis=0,
    )
    enc_last()

    tok_rows = enc_own.shape[0]
    group = 32 // tok_rows

    def unpack(j, carry):
        block = enc_all[pl.ds(j * group, group), :, wide_a:3 * wide_a].astype(jnp.float32)
        enc_rows[pl.ds(pl.multiple_of(j * 32, 32), 32), :] = block.reshape(32, -1).astype(jnp.bfloat16)
        return carry

    lax.fori_loop(0, n // group, unpack, 0)
    each_tile = TILE_LEN // tok_rows

    def own_tile(cols):
        rows = None
        for t in range(n // each_tile):
            there = enc_all[t * each_tile:(t + 1) * each_tile, :, cols].astype(jnp.float32)
            there = there.reshape(TILE_LEN, -1)
            if rows is None:
                rows, chosen = there, jnp.broadcast_to(tile_own[0], there.shape)
            else:
                rows = jnp.where(chosen == t, there, rows)
        return rows

    queries = own_tile(slice(0, wide_a)).astype(jnp.bfloat16)
    columns = [None] * (wide_a // HD)
    scored = []
    for h in range(EH):
        low, high = h * EHD // HD, (h * EHD + EHD - 1) // HD + 1
        span = slice(low * HD, high * HD)
        lane = lax.broadcasted_iota(jnp.int32, (1, (high - low) * HD), 1) + low * HD
        inside = (lane >= h * EHD) & (lane < (h + 1) * EHD)
        picked = jnp.where(inside, queries[:, span], jnp.zeros((), jnp.bfloat16))
        scores = lax.dot_general(
            picked, enc_rows[:, span], (((1,), (1,)), ((), ())), preferred_element_type=jnp.float32
        )
        scored.append((low, high, inside, scores))
    for low, high, inside, scores in scored:
        powers = jnp.exp2((scores - jnp.max(scores, axis=-1, keepdims=True)) * (EHD ** (-0.5) * LOG2E))
        weights = (powers * (1.0 / jnp.sum(powers, axis=-1, keepdims=True))).astype(jnp.bfloat16)
        part = jnp.dot(
            weights, enc_rows[:, wide_a + low * HD:wide_a + high * HD], preferred_element_type=jnp.float32
        )
        for b in range(low, high):
            here = slice((b - low) * HD, (b - low + 1) * HD)
            columns[b] = part[:, here] if columns[b] is None else jnp.where(inside[:, here], part[:, here], columns[b])
    enc_attn = jnp.concatenate(columns, axis=1).astype(jnp.bfloat16)
    loads[1].wait()
    resid = own_tile(slice(3 * wide_a, enc_own.shape[1])) + jnp.dot(
        enc_attn, weo[...], preferred_element_type=jnp.float32
    )
    features = layer_norm(resid).astype(jnp.bfloat16)
    loads[2].wait()

    new_kv[...] = jnp.dot(features, wkv[...], preferred_element_type=jnp.float32).astype(jnp.bfloat16)
    new = jnp.concatenate(
        [
            lax.dot_general(
                query[g * each:(g + 1) * each, :], new_kv[:, g * HD:(g + 1) * HD],
                flip, preferred_element_type=jnp.float32,
            )
            for g in range(kv_heads)
        ],
        axis=0,
    ) * scale
    top = jnp.maximum(old_top, jnp.max(new, axis=-1, keepdims=True))
    new = jnp.exp2(new - top)
    keep = jnp.exp2(old_top - top)
    share = 1.0 / (jnp.sum(new, axis=-1, keepdims=True) + old_total * keep)
    new = (new * share).astype(jnp.bfloat16)
    new_attn = jnp.concatenate(
        [
            jnp.dot(
                new[g * each:(g + 1) * each, :], new_kv[:, width + g * HD:width + (g + 1) * HD],
                preferred_element_type=jnp.float32,
            )
            for g in range(kv_heads)
        ],
        axis=0,
    )
    dec_attn = (old_attn * (keep * share) + new_attn).astype(jnp.bfloat16)
    attn_own[...] = dec_attn
    attn_all[me] = dec_attn
    widen(attn_all, me)
    attn_first, attn_second, attn_third, attn_fourth, attn_last, attn_drain = gather(
        attn_own, attn_all, attn_send, attn_recv, False, widen
    )
    attn_first()
    attn_second()
    attn_third()
    attn_fourth()
    attn_last()
    loads[4].wait()
    scatter(project(wo), o_out, o_in, o_send, o_recv)
    norm_drain()
    enc_drain()
    attn_drain()
    collect(o_out, o_in, o_send, o_recv)
    result = (x_rows[...] + head_rows[...]).astype(jnp.bfloat16)
    for k in range(heads):
        out_ref[:, k * HD:(k + 1) * HD] = result[k:k + 1, :]


def fused(n, enc_x, enc_qkv, w_eo, w_kv, dec_x, w_q, w_o, cache_kv, doc_tile, cached_count):
    tok_rows = enc_x.shape[0]
    packed = (tok_rows, enc_qkv.shape[1] * enc_qkv.shape[2] + enc_x.shape[1])
    heads = dec_x.shape[1] // HD
    tokens = n * tok_rows
    bf16, f32 = jnp.bfloat16, jnp.float32
    vmem = pl.BlockSpec(memory_space=pltpu.VMEM)
    hbm = pl.BlockSpec(memory_space=pl.ANY)
    dma = pltpu.SemaphoreType.DMA
    marks = n // 2
    piece = [pltpu.VMEM((heads, HD), bf16), pltpu.VMEM((n, heads, HD), bf16), dma((1,)), dma((marks,))]
    trade = [pltpu.VMEM((n, 2, HD), f32), pltpu.VMEM((n, 2, HD), f32), dma((1,)), dma((1,))]
    return pl.pallas_call(
        functools.partial(fused_kernel, n),
        out_shape=jax.ShapeDtypeStruct(dec_x.shape, bf16),
        in_specs=[hbm] * 10,
        out_specs=vmem,
        scratch_shapes=[
            pltpu.VMEM(w_eo.shape, bf16),
            pltpu.VMEM(w_kv.shape, bf16),
            pltpu.VMEM(w_q.shape, bf16),
            pltpu.VMEM(w_o.shape, bf16),
            pltpu.VMEM(cache_kv.shape[1:], bf16),
            dma((12,)),
            pltpu.VMEM(dec_x.shape, bf16),
            pltpu.SMEM((1,), jnp.int32),
            pltpu.SMEM((1,), jnp.int32),
            pltpu.VMEM(packed, bf16),
            pltpu.VMEM((n,) + packed, bf16),
            dma((1,)),
            dma((marks,)),
            pltpu.VMEM((tokens, 2 * enc_qkv.shape[2]), bf16),
            pltpu.VMEM((TILE_LEN, w_kv.shape[1]), bf16),
            pltpu.VMEM((heads, HD), f32),
            *piece,
            *piece,
            pltpu.VMEM((n * (heads + 8), HD), f32),
            pltpu.VMEM((heads, HD), f32),
            *trade,
            *trade,
        ],
        compiler_params=pltpu.CompilerParams(collective_id=0, has_side_effects=True),
    )(enc_qkv.transpose(1, 0, 2), enc_x, dec_x, doc_tile, cached_count, w_eo, w_kv, w_q, w_o, cache_kv[0])

def solution(mesh):
    n = mesh.shape["seq"]
    return jax.shard_map(
        functools.partial(fused, n) if n == 32 else local,
        mesh=mesh,
        in_specs=(
            P(("group", "seq"), None),
            P(("group", "seq"), None, None),
            P(),
            P(),
            P(("group", "seq"), None),
            P(None, "seq"),
            P(None, "seq"),
            P(("group", "seq"), None, None, None),
            P(("group", "seq")),
            P(("group", "seq")),
        ),
        out_specs=P(("group", "seq"), None),
        check_vma=False,
    )
```

```python
import functools

import jax
import jax.numpy as jnp
from jax import lax
from jax.experimental import pallas as pl
from jax.experimental.pallas import tpu as pltpu
from jax.sharding import PartitionSpec as P

EH = 8
EHD = 80
HD = 128
TILE_LEN = 128
MESH = pl.DeviceIdType.MESH
LOG2E = 1.4426950408889634


def layer_norm(values):
    center = values - jnp.mean(values, axis=-1, keepdims=True)
    spread = jnp.mean(center * center, axis=-1, keepdims=True)
    return center * lax.rsqrt(spread + 1e-05)


def doc_attend(query_row, doc_kv, filled):
    length = doc_kv.shape[0]
    width = doc_kv.shape[1] // 2
    kv_heads = width // HD
    query_heads = query_row.reshape(kv_heads, -1, HD)
    key_heads = doc_kv[:, :width].reshape(length, kv_heads, HD)
    value_heads = doc_kv[:, width:].reshape(length, kv_heads, HD)
    scores = jnp.einsum(
        "gqd,kgd->gqk", query_heads, key_heads, preferred_element_type=jnp.float32
    ) * HD ** (-0.5)
    inside = jnp.arange(length, dtype=jnp.int32) // TILE_LEN <= filled
    scores = jnp.where(inside[None, None, :], scores, -jnp.inf)
    weights = jax.nn.softmax(scores, axis=-1).astype(jnp.bfloat16)
    result = jnp.einsum("gqk,kgd->gqd", weights, value_heads, preferred_element_type=jnp.float32)
    return result.reshape(1, -1).astype(jnp.bfloat16)


def local(enc_x, enc_qkv, w_eo, w_kv, dec_x, w_q, w_o, cache_kv, doc_tile, cached_count):
    tok_rows = enc_x.shape[0]
    query_heads = enc_qkv[:, 0].reshape(tok_rows, EH, EHD)
    key_piece = lax.all_gather(enc_qkv[:, 1], "seq", axis=0, tiled=True)
    value_piece = lax.all_gather(enc_qkv[:, 2], "seq", axis=0, tiled=True)
    length = key_piece.shape[0]
    key_heads = key_piece.reshape(length, EH, EHD)
    value_heads = value_piece.reshape(length, EH, EHD)
    scores = jnp.einsum(
        "qhd,khd->hqk", query_heads, key_heads, preferred_element_type=jnp.float32
    ) * EHD ** (-0.5)
    old_max = jnp.full((EH, tok_rows), -1e30, jnp.float32)
    new_max = jnp.maximum(old_max, jnp.max(scores, axis=-1))
    powers = jnp.exp(scores - new_max[:, :, None])
    new_total = jnp.sum(powers, axis=-1)
    new_acc = jnp.einsum(
        "hqk,khd->hqd", powers.astype(jnp.bfloat16), value_heads, preferred_element_type=jnp.float32
    )
    enc_attn = (
        (new_acc / new_total[:, :, None])
        .transpose(1, 0, 2)
        .reshape(tok_rows, -1)
        .astype(jnp.bfloat16)
    )
    resid = enc_x.astype(jnp.float32) + jnp.dot(enc_attn, w_eo, preferred_element_type=jnp.float32)
    features = layer_norm(resid).astype(jnp.bfloat16)
    tile_start = doc_tile[0] * TILE_LEN
    x_float = dec_x.astype(jnp.float32)
    normed = (
        x_float * lax.rsqrt(jnp.mean(x_float * x_float, axis=-1, keepdims=True) + 1e-05)
    ).astype(jnp.bfloat16)
    query_cols = jnp.dot(
        lax.all_gather(normed, "seq", axis=0, tiled=True), w_q, preferred_element_type=jnp.float32
    ).astype(jnp.bfloat16)
    query_row = lax.all_to_all(query_cols, "seq", split_axis=0, concat_axis=1, tiled=True)
    zero = jnp.zeros((), jnp.int32)
    filled = cached_count[0]
    local_kv = jnp.dot(features, w_kv, preferred_element_type=jnp.float32).astype(jnp.bfloat16)
    buffer = jnp.zeros((TILE_LEN, w_kv.shape[1]), jnp.bfloat16)
    piece = lax.all_gather(local_kv, "seq", axis=0, tiled=True)
    length = piece.shape[0]
    position = jnp.arange(length, dtype=jnp.int32) - tile_start
    inside = (position >= 0) & (position < buffer.shape[0])
    clipped = jnp.clip(position, 0, buffer.shape[0] - 1)
    tile_kv = buffer.at[clipped].add(jnp.where(inside[:, None], piece, jnp.zeros_like(piece)))
    doc_kv = lax.dynamic_update_slice(cache_kv[0], tile_kv[None], (filled, zero, zero))
    doc_kv = doc_kv.reshape(-1, doc_kv.shape[-1])
    dec_attn = doc_attend(query_row[0], doc_kv, filled)
    output_cols = jnp.dot(
        lax.all_gather(dec_attn, "seq", axis=0, tiled=True), w_o, preferred_element_type=jnp.float32
    ).astype(jnp.bfloat16)
    attn_out = lax.all_to_all(output_cols, "seq", split_axis=0, concat_axis=1, tiled=True)
    return (x_float + attn_out.astype(jnp.float32)).astype(jnp.bfloat16)


def fused_kernel(
    n, qkv_hbm, resid_hbm, x_hbm, tile_hbm, count_hbm, weo_hbm, wkv_hbm, wq_hbm, wo_hbm, cache_hbm, out_ref,
    weo, wkv, wq, wo, cache, load_sem, x_own, tile_own, count_own,
    enc_own, enc_all, enc_send, enc_recv, res_own, res_all, res_send, res_recv, enc_rows, new_kv,
    x_rows, norm_own, norm_all, norm_send, norm_recv,
    attn_own, attn_all, attn_send, attn_recv,
    wide, head_rows,
    q_out, q_in, q_send, q_recv,
    o_out, o_in, o_send, o_recv,
):
    me = lax.axis_index("seq")
    inner = 4
    outer = n // (2 * inner)
    zi, qi, ci = me // (2 * inner), (me // 2) % inner, me % 2

    def at(kz, kq, kc):
        return (zi + kz) % outer * (2 * inner) + (qi + kq) % inner * 2 + (ci + kc) % 2

    barrier = pltpu.get_barrier_semaphore()

    partners = [at(kz, 0, 0) for kz in range(1, outer)] + [at(0, kq, 0) for kq in range(1, inner)] + [at(0, 0, 1)]
    for partner in partners:
        pl.semaphore_signal(barrier, inc=1, device_id={"seq": partner}, device_id_type=MESH)

    wide_a = EH * EHD
    heads = x_rows.shape[0]
    pitch = wide.shape[0] // n

    def widen(every, slot):
        wide[pl.ds(pl.multiple_of(slot * pitch, 8), heads), :] = every[slot].astype(jnp.float32)

    small = [
        pltpu.make_async_copy(src, dst, load_sem.at[5 + i])
        for i, (src, dst) in enumerate(
            [(x_hbm, x_own)]
            + [(qkv_hbm.at[j], enc_own.at[:, pl.ds(j * wide_a, wide_a)]) for j in range(3)]
            + [(resid_hbm, res_own)]
            + [(tile_hbm, tile_own), (count_hbm, count_own)]
        )
    ]
    for load in small:
        load.start()
    loads = [
        pltpu.make_async_copy(src, dst, load_sem.at[i])
        for i, (src, dst) in enumerate(
            ((wq_hbm, wq), (weo_hbm, weo), (wkv_hbm, wkv), (cache_hbm, cache), (wo_hbm, wo))
        )
    ]
    for load in loads:
        load.start()

    small[0].wait()
    for k in range(heads):
        x_rows[k:k + 1, :] = x_own[:, k * HD:(k + 1) * HD].astype(jnp.float32)
    x_float = x_rows[...]
    squares = jnp.sum(jnp.sum(x_float * x_float, axis=1, keepdims=True), axis=0, keepdims=True)
    normed = (x_float * lax.rsqrt(squares / x_float.size + 1e-05)).astype(jnp.bfloat16)
    norm_own[...] = normed
    norm_all[me] = normed
    widen(norm_all, me)
    for load in small[1:]:
        load.wait()
    enc_all[me] = enc_own[...]
    res_all[me] = res_own[...]
    pl.semaphore_wait(barrier, len(partners))

    flip_x = qi + 1 - 2 * (qi % 2)
    flip_y = (qi + 2) % inner
    flip_both = (flip_x + 2) % inner

    def place(kz, plane, core):
        return (zi + kz + outer) % outer * (2 * inner) + plane * 2 + core

    def gather(own, every, send, recv, relay, ready):
        near, side, far, core = 0, (outer - 1, 2 * outer - 1), 3 * outer - 1, 4 * outer - 1

        def copy(src, slot, mark, device):
            return pltpu.make_async_remote_copy(
                src_ref=src, dst_ref=every.at[slot], send_sem=send.at[0], recv_sem=recv.at[mark],
                device_id={"seq": device}, device_id_type=MESH,
            )

        def push(src, slot, mark, device):
            copy(src, slot, mark, device).start()

        def take(slot, mark):
            copy(own, slot, mark, place(0, qi, 1 - ci)).wait_recv()

        def spread(src, slot, kz):
            if not relay:
                push(src, slot, far + kz, place(0, flip_both, ci))
            push(src, slot, side[0] + kz, place(0, flip_x, ci))
            push(src, slot, side[1] + kz, place(0, flip_y, ci))
            push(src, slot, core, place(0, qi, 1 - ci))

        def first(along=True, across=True):
            if along:
                for kz in range(1, outer):
                    push(own, me, near + kz - 1, place(kz, qi, ci))
            if across:
                spread(own, me, 0)

        def second(steps=range(1, outer)):
            for kz in steps:
                slot = place(-kz, qi, ci)
                take(slot, near + kz - 1)
                spread(every.at[slot], slot, kz)
                ready(every, slot)

        def third(steps=range(outer)):
            for kz in steps:
                for odd, (plane, onward) in enumerate(((flip_x, flip_y), (flip_y, flip_x))):
                    slot = place(-kz, plane, ci)
                    take(slot, side[odd] + kz)
                    if relay and kz % 2 == odd:
                        push(every.at[slot], slot, far + kz, place(0, onward, ci))
                    push(every.at[slot], slot, core, place(0, qi, 1 - ci))
                    ready(every, slot)

        def fourth(steps=range(outer)):
            for kz in steps:
                slot = place(-kz, flip_both, ci)
                take(slot, far + kz)
                push(every.at[slot], slot, core, place(0, qi, 1 - ci))
                ready(every, slot)

        def last():
            half = every.at[pl.ds(0, n // 2)]
            copy(half, pl.ds(0, n // 2), core, place(0, qi, 1 - ci)).wait_recv()
            for pair in range(n // 2):
                ready(every, 2 * pair + 1 - ci)

        def drain():
            most = every.at[pl.ds(0, n - 1)]
            copy(most, pl.ds(0, n - 1), core, place(0, qi, 1 - ci)).wait_send()

        return first, second, third, fourth, last, drain

    def scatter(values, out, into, send, recv):
        rounded = values.astype(jnp.bfloat16).astype(jnp.float32)
        for d in range(n):
            for half in range(2):
                out[d, half:half + 1, :] = rounded[d:d + 1, half * HD:(half + 1) * HD]

        def one(k, carry):
            device = (me + k) % n
            pltpu.make_async_remote_copy(
                src_ref=out.at[device], dst_ref=into.at[me], send_sem=send.at[0], recv_sem=recv.at[0],
                device_id={"seq": device}, device_id_type=MESH,
            ).start()
            return carry

        lax.fori_loop(1, n, one, 0)
        into[me] = out[me]

    def collect(out, into, send, recv):
        copy = pltpu.make_async_remote_copy(
            src_ref=out.at[pl.ds(0, n - 1)], dst_ref=into.at[pl.ds(0, n - 1)], send_sem=send.at[0], recv_sem=recv.at[0],
            device_id={"seq": place(0, qi, 1 - ci)}, device_id_type=MESH,
        )
        copy.wait_recv()
        copy.wait_send()
        for d in range(n):
            head_rows[2 * d:2 * d + 2, :] = into[d]

    def project(weight):
        total = None
        for k in range(0, heads, 2):
            pair = [wide[pl.ds(k + j, n, stride=pitch), :] for j in range(2)]
            term = jnp.dot(
                jnp.concatenate(pair, axis=1).astype(jnp.bfloat16), weight[k * HD:(k + 2) * HD, :],
                preferred_element_type=jnp.float32,
            )
            total = term if total is None else total + term
        return total

    norm_first, norm_second, norm_third, norm_fourth, norm_last, norm_drain = gather(
        norm_own, norm_all, norm_send, norm_recv, False, widen
    )
    enc_first, enc_second, enc_third, enc_fourth, enc_last, enc_drain = gather(
        enc_own, enc_all, enc_send, enc_recv, False, lambda every, slot: None
    )
    res_first, res_second, res_third, res_fourth, res_last, res_drain = gather(
        res_own, res_all, res_send, res_recv, True, lambda every, slot: None
    )
    norm_first()
    enc_first()
    res_first()
    norm_second()
    enc_second()
    res_second()
    norm_third()
    norm_fourth()
    norm_last()
    loads[0].wait()
    scatter(project(wq), q_out, q_in, q_send, q_recv)
    enc_third()
    enc_fourth()
    res_third()
    enc_last()

    tok_rows = enc_own.shape[0]
    group = 32 // tok_rows

    def unpack(j, carry):
        block = enc_all[pl.ds(j * group, group), :, wide_a:3 * wide_a].astype(jnp.float32)
        enc_rows[pl.ds(pl.multiple_of(j * 32, 32), 32), :] = block.reshape(32, -1).astype(jnp.bfloat16)
        return carry

    lax.fori_loop(0, n // group, unpack, 0)
    each_tile = TILE_LEN // tok_rows

    def own_tile(every, cols):
        rows = None
        for t in range(n // each_tile):
            there = every[t * each_tile:(t + 1) * each_tile, :, cols].astype(jnp.float32)
            there = there.reshape(TILE_LEN, -1)
            if rows is None:
                rows, chosen = there, jnp.broadcast_to(tile_own[0], there.shape)
            else:
                rows = jnp.where(chosen == t, there, rows)
        return rows

    queries = own_tile(enc_all, slice(0, wide_a)).astype(jnp.bfloat16)
    columns = [None] * (wide_a // HD)
    scored = []
    for h in range(EH):
        low, high = h * EHD // HD, (h * EHD + EHD - 1) // HD + 1
        span = slice(low * HD, high * HD)
        lane = lax.broadcasted_iota(jnp.int32, (1, (high - low) * HD), 1) + low * HD
        inside = (lane >= h * EHD) & (lane < (h + 1) * EHD)
        picked = jnp.where(inside, queries[:, span], jnp.zeros((), jnp.bfloat16))
        scores = lax.dot_general(
            picked, enc_rows[:, span], (((1,), (1,)), ((), ())), preferred_element_type=jnp.float32
        )
        scored.append((low, high, inside, scores))
    for low, high, inside, scores in scored:
        powers = jnp.exp2((scores - jnp.max(scores, axis=-1, keepdims=True)) * (EHD ** (-0.5) * LOG2E))
        weights = (powers * (1.0 / jnp.sum(powers, axis=-1, keepdims=True))).astype(jnp.bfloat16)
        part = jnp.dot(
            weights, enc_rows[:, wide_a + low * HD:wide_a + high * HD], preferred_element_type=jnp.float32
        )
        for b in range(low, high):
            here = slice((b - low) * HD, (b - low + 1) * HD)
            columns[b] = part[:, here] if columns[b] is None else jnp.where(inside[:, here], part[:, here], columns[b])
    enc_attn = jnp.concatenate(columns, axis=1).astype(jnp.bfloat16)
    res_fourth()
    loads[3].wait()
    collect(q_out, q_in, q_send, q_recv)
    width = new_kv.shape[1] // 2
    kv_heads = width // HD
    each = heads // kv_heads
    flip = (((1,), (1,)), ((), ()))
    scale = HD ** (-0.5) * LOG2E
    query = head_rows[...].astype(jnp.bfloat16)
    old = jnp.concatenate(
        [
            lax.dot_general(
                query[g * each:(g + 1) * each, :], cache[:, :, g * HD:(g + 1) * HD].reshape(-1, HD),
                flip, preferred_element_type=jnp.float32,
            )
            for g in range(kv_heads)
        ],
        axis=0,
    ) * scale
    token = lax.broadcasted_iota(jnp.int32, old.shape, 1)
    cached = token // TILE_LEN < jnp.broadcast_to(count_own[0], token.shape)
    old = jnp.where(cached, old, -jnp.inf)
    old_top = jnp.max(old, axis=-1, keepdims=True)
    old = jnp.where(cached, jnp.exp2(old - old_top), 0.0)
    old_total = jnp.sum(old, axis=-1, keepdims=True)
    old = old.astype(jnp.bfloat16)
    old_attn = jnp.concatenate(
        [
            jnp.dot(
                old[g * each:(g + 1) * each, :], cache[:, :, width + g * HD:width + (g + 1) * HD].reshape(-1, HD),
                preferred_element_type=jnp.float32,
            )
            for g in range(kv_heads)
        ],
        axis=0,
    )
    res_last()
    loads[1].wait()
    resid = own_tile(res_all, slice(0, res_own.shape[1])) + jnp.dot(
        enc_attn, weo[...], preferred_element_type=jnp.float32
    )
    features = layer_norm(resid).astype(jnp.bfloat16)

    loads[2].wait()
    new_kv[...] = jnp.dot(features, wkv[...], preferred_element_type=jnp.float32).astype(jnp.bfloat16)
    new = jnp.concatenate(
        [
            lax.dot_general(
                query[g * each:(g + 1) * each, :], new_kv[:, g * HD:(g + 1) * HD],
                flip, preferred_element_type=jnp.float32,
            )
            for g in range(kv_heads)
        ],
        axis=0,
    ) * scale
    top = jnp.maximum(old_top, jnp.max(new, axis=-1, keepdims=True))
    new = jnp.exp2(new - top)
    keep = jnp.exp2(old_top - top)
    share = 1.0 / (jnp.sum(new, axis=-1, keepdims=True) + old_total * keep)
    new = (new * share).astype(jnp.bfloat16)
    new_attn = jnp.concatenate(
        [
            jnp.dot(
                new[g * each:(g + 1) * each, :], new_kv[:, width + g * HD:width + (g + 1) * HD],
                preferred_element_type=jnp.float32,
            )
            for g in range(kv_heads)
        ],
        axis=0,
    )
    dec_attn = (old_attn * (keep * share) + new_attn).astype(jnp.bfloat16)
    attn_own[...] = dec_attn
    attn_all[me] = dec_attn
    widen(attn_all, me)
    attn_first, attn_second, attn_third, attn_fourth, attn_last, attn_drain = gather(
        attn_own, attn_all, attn_send, attn_recv, False, widen
    )
    attn_first()
    attn_second()
    attn_third()
    attn_fourth()
    attn_last()
    loads[4].wait()
    scatter(project(wo), o_out, o_in, o_send, o_recv)
    norm_drain()
    enc_drain()
    res_drain()
    attn_drain()
    collect(o_out, o_in, o_send, o_recv)
    result = (x_rows[...] + head_rows[...]).astype(jnp.bfloat16)
    for k in range(heads):
        out_ref[:, k * HD:(k + 1) * HD] = result[k:k + 1, :]


def fused(n, enc_x, enc_qkv, w_eo, w_kv, dec_x, w_q, w_o, cache_kv, doc_tile, cached_count):
    tok_rows = enc_x.shape[0]
    packed = (tok_rows, enc_qkv.shape[1] * enc_qkv.shape[2])
    heads = dec_x.shape[1] // HD
    tokens = n * tok_rows
    bf16, f32 = jnp.bfloat16, jnp.float32
    vmem = pl.BlockSpec(memory_space=pltpu.VMEM)
    hbm = pl.BlockSpec(memory_space=pl.ANY)
    dma = pltpu.SemaphoreType.DMA
    marks = n // 2
    piece = [pltpu.VMEM((heads, HD), bf16), pltpu.VMEM((n, heads, HD), bf16), dma((1,)), dma((marks,))]
    trade = [pltpu.VMEM((n, 2, HD), f32), pltpu.VMEM((n, 2, HD), f32), dma((1,)), dma((1,))]
    return pl.pallas_call(
        functools.partial(fused_kernel, n),
        out_shape=pltpu.VMEM(dec_x.shape, bf16),
        in_specs=[hbm] * 10,
        out_specs=vmem,
        scratch_shapes=[
            pltpu.VMEM(w_eo.shape, bf16),
            pltpu.VMEM(w_kv.shape, bf16),
            pltpu.VMEM(w_q.shape, bf16),
            pltpu.VMEM(w_o.shape, bf16),
            pltpu.VMEM(cache_kv.shape[1:], bf16),
            dma((12,)),
            pltpu.VMEM(dec_x.shape, bf16),
            pltpu.SMEM((1,), jnp.int32),
            pltpu.SMEM((1,), jnp.int32),
            pltpu.VMEM(packed, bf16),
            pltpu.VMEM((n,) + packed, bf16),
            dma((1,)),
            dma((marks,)),
            pltpu.VMEM(enc_x.shape, bf16),
            pltpu.VMEM((n,) + enc_x.shape, bf16),
            dma((1,)),
            dma((marks,)),
            pltpu.VMEM((tokens, 2 * enc_qkv.shape[2]), bf16),
            pltpu.VMEM((TILE_LEN, w_kv.shape[1]), bf16),
            pltpu.VMEM((heads, HD), f32),
            *piece,
            *piece,
            pltpu.VMEM((n * (heads + 8), HD), f32),
            pltpu.VMEM((heads, HD), f32),
            *trade,
            *trade,
        ],
        compiler_params=pltpu.CompilerParams(collective_id=0, has_side_effects=True),
    )(enc_qkv.transpose(1, 0, 2), enc_x, dec_x, doc_tile, cached_count, w_eo, w_kv, w_q, w_o, cache_kv[0])

def solution(mesh):
    n = mesh.shape["seq"]
    return jax.shard_map(
        functools.partial(fused, n) if n == 32 else local,
        mesh=mesh,
        in_specs=(
            P(("group", "seq"), None),
            P(("group", "seq"), None, None),
            P(),
            P(),
            P(("group", "seq"), None),
            P(None, "seq"),
            P(None, "seq"),
            P(("group", "seq"), None, None, None),
            P(("group", "seq")),
            P(("group", "seq")),
        ),
        out_specs=P(("group", "seq"), None),
        check_vma=False,
    )
```

```python
import functools

import jax
import jax.numpy as jnp
from jax import lax
from jax.experimental import pallas as pl
from jax.experimental.pallas import tpu as pltpu
from jax.sharding import PartitionSpec as P

EH = 8
EHD = 80
HD = 128
TILE_LEN = 128
MESH = pl.DeviceIdType.MESH
LOG2E = 1.4426950408889634


def layer_norm(values):
    center = values - jnp.mean(values, axis=-1, keepdims=True)
    spread = jnp.mean(center * center, axis=-1, keepdims=True)
    return center * lax.rsqrt(spread + 1e-05)


def doc_attend(query_row, doc_kv, filled):
    length = doc_kv.shape[0]
    width = doc_kv.shape[1] // 2
    kv_heads = width // HD
    query_heads = query_row.reshape(kv_heads, -1, HD)
    key_heads = doc_kv[:, :width].reshape(length, kv_heads, HD)
    value_heads = doc_kv[:, width:].reshape(length, kv_heads, HD)
    scores = jnp.einsum(
        "gqd,kgd->gqk", query_heads, key_heads, preferred_element_type=jnp.float32
    ) * HD ** (-0.5)
    inside = jnp.arange(length, dtype=jnp.int32) // TILE_LEN <= filled
    scores = jnp.where(inside[None, None, :], scores, -jnp.inf)
    weights = jax.nn.softmax(scores, axis=-1).astype(jnp.bfloat16)
    result = jnp.einsum("gqk,kgd->gqd", weights, value_heads, preferred_element_type=jnp.float32)
    return result.reshape(1, -1).astype(jnp.bfloat16)


def local(enc_x, enc_qkv, w_eo, w_kv, dec_x, w_q, w_o, cache_kv, doc_tile, cached_count):
    tok_rows = enc_x.shape[0]
    query_heads = enc_qkv[:, 0].reshape(tok_rows, EH, EHD)
    key_piece = lax.all_gather(enc_qkv[:, 1], "seq", axis=0, tiled=True)
    value_piece = lax.all_gather(enc_qkv[:, 2], "seq", axis=0, tiled=True)
    length = key_piece.shape[0]
    key_heads = key_piece.reshape(length, EH, EHD)
    value_heads = value_piece.reshape(length, EH, EHD)
    scores = jnp.einsum(
        "qhd,khd->hqk", query_heads, key_heads, preferred_element_type=jnp.float32
    ) * EHD ** (-0.5)
    old_max = jnp.full((EH, tok_rows), -1e30, jnp.float32)
    new_max = jnp.maximum(old_max, jnp.max(scores, axis=-1))
    powers = jnp.exp(scores - new_max[:, :, None])
    new_total = jnp.sum(powers, axis=-1)
    new_acc = jnp.einsum(
        "hqk,khd->hqd", powers.astype(jnp.bfloat16), value_heads, preferred_element_type=jnp.float32
    )
    enc_attn = (
        (new_acc / new_total[:, :, None])
        .transpose(1, 0, 2)
        .reshape(tok_rows, -1)
        .astype(jnp.bfloat16)
    )
    resid = enc_x.astype(jnp.float32) + jnp.dot(enc_attn, w_eo, preferred_element_type=jnp.float32)
    features = layer_norm(resid).astype(jnp.bfloat16)
    tile_start = doc_tile[0] * TILE_LEN
    x_float = dec_x.astype(jnp.float32)
    normed = (
        x_float * lax.rsqrt(jnp.mean(x_float * x_float, axis=-1, keepdims=True) + 1e-05)
    ).astype(jnp.bfloat16)
    query_cols = jnp.dot(
        lax.all_gather(normed, "seq", axis=0, tiled=True), w_q, preferred_element_type=jnp.float32
    ).astype(jnp.bfloat16)
    query_row = lax.all_to_all(query_cols, "seq", split_axis=0, concat_axis=1, tiled=True)
    zero = jnp.zeros((), jnp.int32)
    filled = cached_count[0]
    local_kv = jnp.dot(features, w_kv, preferred_element_type=jnp.float32).astype(jnp.bfloat16)
    buffer = jnp.zeros((TILE_LEN, w_kv.shape[1]), jnp.bfloat16)
    piece = lax.all_gather(local_kv, "seq", axis=0, tiled=True)
    length = piece.shape[0]
    position = jnp.arange(length, dtype=jnp.int32) - tile_start
    inside = (position >= 0) & (position < buffer.shape[0])
    clipped = jnp.clip(position, 0, buffer.shape[0] - 1)
    tile_kv = buffer.at[clipped].add(jnp.where(inside[:, None], piece, jnp.zeros_like(piece)))
    doc_kv = lax.dynamic_update_slice(cache_kv[0], tile_kv[None], (filled, zero, zero))
    doc_kv = doc_kv.reshape(-1, doc_kv.shape[-1])
    dec_attn = doc_attend(query_row[0], doc_kv, filled)
    output_cols = jnp.dot(
        lax.all_gather(dec_attn, "seq", axis=0, tiled=True), w_o, preferred_element_type=jnp.float32
    ).astype(jnp.bfloat16)
    attn_out = lax.all_to_all(output_cols, "seq", split_axis=0, concat_axis=1, tiled=True)
    return (x_float + attn_out.astype(jnp.float32)).astype(jnp.bfloat16)


def fused_kernel(
    n, qkv_hbm, resid_hbm, x_hbm, tile_hbm, count_hbm, weo_hbm, wkv_hbm, wq_hbm, wo_hbm, cache_hbm, out_ref,
    weo, wkv, wq, wo, cache, load_sem, x_own, tile_own, count_own,
    enc_own, enc_all, enc_send, enc_recv, res_own, res_all, res_send, res_recv, enc_rows, new_kv,
    x_rows, norm_own, norm_all, norm_send, norm_recv,
    attn_own, attn_all, attn_send, attn_recv,
    wide, head_rows,
    q_out, q_in, q_send, q_recv,
    o_out, o_in, o_send, o_recv,
):
    me = lax.axis_index("seq")
    inner = 4
    outer = n // (2 * inner)
    zi, qi, ci = me // (2 * inner), (me // 2) % inner, me % 2

    def at(kz, kq, kc):
        return (zi + kz) % outer * (2 * inner) + (qi + kq) % inner * 2 + (ci + kc) % 2

    barrier = pltpu.get_barrier_semaphore()

    partners = [at(kz, 0, 0) for kz in range(1, outer)] + [at(0, kq, 0) for kq in range(1, inner)] + [at(0, 0, 1)]
    for partner in partners:
        pl.semaphore_signal(barrier, inc=1, device_id={"seq": partner}, device_id_type=MESH)

    wide_a = EH * EHD
    heads = x_rows.shape[0]
    pitch = wide.shape[0] // n

    def widen(every, slot):
        wide[pl.ds(pl.multiple_of(slot * pitch, 8), heads), :] = every[slot].astype(jnp.float32)

    small = [
        pltpu.make_async_copy(src, dst, load_sem.at[5 + i])
        for i, (src, dst) in enumerate(
            [(x_hbm, x_own)]
            + [(qkv_hbm.at[j], enc_own.at[:, pl.ds(j * wide_a, wide_a)]) for j in range(3)]
            + [(resid_hbm, res_own)]
            + [(tile_hbm, tile_own), (count_hbm, count_own)]
        )
    ]
    for load in small:
        load.start()
    loads = [
        pltpu.make_async_copy(src, dst, load_sem.at[i])
        for i, (src, dst) in enumerate(
            ((wq_hbm, wq), (weo_hbm, weo), (wkv_hbm, wkv), (cache_hbm, cache), (wo_hbm, wo))
        )
    ]
    for load in loads:
        load.start()

    small[0].wait()
    for k in range(heads):
        x_rows[k:k + 1, :] = x_own[:, k * HD:(k + 1) * HD].astype(jnp.float32)
    x_float = x_rows[...]
    squares = jnp.sum(jnp.sum(x_float * x_float, axis=1, keepdims=True), axis=0, keepdims=True)
    normed = (x_float * lax.rsqrt(squares / x_float.size + 1e-05)).astype(jnp.bfloat16)
    norm_own[...] = normed
    norm_all[me] = normed
    widen(norm_all, me)
    for load in small[1:]:
        load.wait()
    enc_all[me] = enc_own[...]
    res_all[me] = res_own[...]
    pl.semaphore_wait(barrier, len(partners))

    flip_x = qi + 1 - 2 * (qi % 2)
    flip_y = (qi + 2) % inner
    flip_both = (flip_x + 2) % inner

    def place(kz, plane, core):
        return (zi + kz + outer) % outer * (2 * inner) + plane * 2 + core

    def gather(own, every, send, recv, relay, ready):
        near, side, far, core = 0, (outer - 1, 2 * outer - 1), 3 * outer - 1, 4 * outer - 1

        def copy(src, slot, mark, device):
            return pltpu.make_async_remote_copy(
                src_ref=src, dst_ref=every.at[slot], send_sem=send.at[0], recv_sem=recv.at[mark],
                device_id={"seq": device}, device_id_type=MESH,
            )

        def push(src, slot, mark, device):
            copy(src, slot, mark, device).start()

        def take(slot, mark):
            copy(own, slot, mark, place(0, qi, 1 - ci)).wait_recv()

        def spread(src, slot, kz):
            if not relay:
                push(src, slot, far + kz, place(0, flip_both, ci))
            push(src, slot, side[0] + kz, place(0, flip_x, ci))
            push(src, slot, side[1] + kz, place(0, flip_y, ci))
            push(src, slot, core, place(0, qi, 1 - ci))

        def first(along=True, across=True):
            if along:
                for kz in range(1, outer):
                    push(own, me, near + kz - 1, place(kz, qi, ci))
            if across:
                spread(own, me, 0)

        def second(steps=range(1, outer)):
            for kz in steps:
                slot = place(-kz, qi, ci)
                take(slot, near + kz - 1)
                spread(every.at[slot], slot, kz)
                ready(every, slot)

        def third(steps=range(outer)):
            for kz in steps:
                for odd, (plane, onward) in enumerate(((flip_x, flip_y), (flip_y, flip_x))):
                    slot = place(-kz, plane, ci)
                    take(slot, side[odd] + kz)
                    if relay and kz % 2 == odd:
                        push(every.at[slot], slot, far + kz, place(0, onward, ci))
                    push(every.at[slot], slot, core, place(0, qi, 1 - ci))
                    ready(every, slot)

        def fourth(steps=range(outer)):
            for kz in steps:
                slot = place(-kz, flip_both, ci)
                take(slot, far + kz)
                push(every.at[slot], slot, core, place(0, qi, 1 - ci))
                ready(every, slot)

        def last():
            half = every.at[pl.ds(0, n // 2)]
            copy(half, pl.ds(0, n // 2), core, place(0, qi, 1 - ci)).wait_recv()
            for pair in range(n // 2):
                ready(every, 2 * pair + 1 - ci)

        def drain():
            most = every.at[pl.ds(0, n - 1)]
            copy(most, pl.ds(0, n - 1), core, place(0, qi, 1 - ci)).wait_send()

        return first, second, third, fourth, last, drain

    def scatter(values, out, into, send, recv):
        rounded = values.astype(jnp.bfloat16).astype(jnp.float32)
        for d in range(n):
            for half in range(2):
                out[d, half:half + 1, :] = rounded[d:d + 1, half * HD:(half + 1) * HD]

        def one(k, carry):
            device = (me + k) % n
            pltpu.make_async_remote_copy(
                src_ref=out.at[device], dst_ref=into.at[me], send_sem=send.at[0], recv_sem=recv.at[0],
                device_id={"seq": device}, device_id_type=MESH,
            ).start()
            return carry

        lax.fori_loop(1, n, one, 0)
        into[me] = out[me]

    def collect(out, into, send, recv):
        copy = pltpu.make_async_remote_copy(
            src_ref=out.at[pl.ds(0, n - 1)], dst_ref=into.at[pl.ds(0, n - 1)], send_sem=send.at[0], recv_sem=recv.at[0],
            device_id={"seq": place(0, qi, 1 - ci)}, device_id_type=MESH,
        )
        copy.wait_recv()
        copy.wait_send()
        for d in range(n):
            head_rows[2 * d:2 * d + 2, :] = into[d]

    def project(weight):
        total = [None, None]
        for k in range(0, heads, 2):
            pair = [wide[pl.ds(k + j, n, stride=pitch), :] for j in range(2)]
            rows = jnp.concatenate(pair, axis=1).astype(jnp.bfloat16)
            for j in range(2):
                term = jnp.dot(
                    rows, weight[k * HD:(k + 2) * HD, j * HD:(j + 1) * HD], preferred_element_type=jnp.float32
                )
                total[j] = term if total[j] is None else total[j] + term
        return jnp.concatenate(total, axis=1)

    norm_first, norm_second, norm_third, norm_fourth, norm_last, norm_drain = gather(
        norm_own, norm_all, norm_send, norm_recv, False, widen
    )
    enc_first, enc_second, enc_third, enc_fourth, enc_last, enc_drain = gather(
        enc_own, enc_all, enc_send, enc_recv, False, lambda every, slot: None
    )
    def plane_gather(own, every, send, recv):
        core, along = inner - 1, inner
        across = (flip_x, flip_y, flip_both)

        def copy(src, to, mark, device):
            return pltpu.make_async_remote_copy(
                src_ref=src, dst_ref=every.at[to], send_sem=send.at[0], recv_sem=recv.at[mark],
                device_id={"seq": device}, device_id_type=MESH,
            )

        def several(count):
            return every.at[pl.ds(0, count)], pl.ds(0, count)

        def first():
            for mark, plane in enumerate(across):
                copy(own, me, mark, place(0, plane, ci)).start()
            copy(own, me, core, place(0, qi, 1 - ci)).start()

        def second():
            for mark, plane in enumerate(across):
                copy(own, place(0, plane, ci), mark, place(0, plane, ci)).wait_recv()
            for kz in range(1, outer):
                copy(own, me, along + kz - 1, place(kz, qi, ci)).start()
            for plane in across:
                slot = place(0, plane, ci)
                for kz in range(1, outer):
                    copy(every.at[slot], slot, along + kz - 1, place(kz, qi, ci)).start()
            for plane in across:
                slot = place(0, plane, ci)
                copy(every.at[slot], slot, core, place(0, qi, 1 - ci)).start()

        def third():
            for kz in range(1, outer):
                copy(*several(inner), along + kz - 1, place(kz, qi, ci)).wait_recv()
                for plane in (qi,) + across:
                    slot = place(-kz, plane, ci)
                    copy(every.at[slot], slot, core, place(0, qi, 1 - ci)).start()

        def last():
            copy(*several(n // 2), core, place(0, qi, 1 - ci)).wait_recv()

        def drain():
            copy(*several(n - 1), core, place(0, qi, 1 - ci)).wait_send()

        return first, second, third, last, drain

    res_first, res_second, res_third, res_last, res_drain = plane_gather(res_own, res_all, res_send, res_recv)
    norm_first()
    enc_first()
    res_first()
    norm_second()
    res_second()
    enc_second()
    norm_third()
    norm_fourth()
    norm_last()
    loads[0].wait()
    scatter(project(wq), q_out, q_in, q_send, q_recv)
    enc_third()
    enc_fourth()
    enc_last()

    tok_rows = enc_own.shape[0]
    group = 32 // tok_rows

    def unpack(j, carry):
        block = enc_all[pl.ds(j * group, group), :, wide_a:3 * wide_a].astype(jnp.float32)
        enc_rows[pl.ds(pl.multiple_of(j * 32, 32), 32), :] = block.reshape(32, -1).astype(jnp.bfloat16)
        return carry

    lax.fori_loop(0, n // group, unpack, 0)
    each_tile = TILE_LEN // tok_rows

    def own_tile(every, cols):
        rows = None
        for t in range(n // each_tile):
            there = every[t * each_tile:(t + 1) * each_tile, :, cols].astype(jnp.float32)
            there = there.reshape(TILE_LEN, -1)
            if rows is None:
                rows, chosen = there, jnp.broadcast_to(tile_own[0], there.shape)
            else:
                rows = jnp.where(chosen == t, there, rows)
        return rows

    queries = own_tile(enc_all, slice(0, wide_a)).astype(jnp.bfloat16)
    columns = [None] * (wide_a // HD)
    scored = []
    for h in range(EH):
        low, high = h * EHD // HD, (h * EHD + EHD - 1) // HD + 1
        span = slice(low * HD, high * HD)
        lane = lax.broadcasted_iota(jnp.int32, (1, (high - low) * HD), 1) + low * HD
        inside = (lane >= h * EHD) & (lane < (h + 1) * EHD)
        picked = jnp.where(inside, queries[:, span], jnp.zeros((), jnp.bfloat16))
        scores = lax.dot_general(
            picked, enc_rows[:, span], (((1,), (1,)), ((), ())), preferred_element_type=jnp.float32
        )
        scored.append((low, high, inside, scores))
    for low, high, inside, scores in scored:
        powers = jnp.exp2((scores - jnp.max(scores, axis=-1, keepdims=True)) * (EHD ** (-0.5) * LOG2E))
        weights = (powers * (1.0 / jnp.sum(powers, axis=-1, keepdims=True))).astype(jnp.bfloat16)
        part = jnp.dot(
            weights, enc_rows[:, wide_a + low * HD:wide_a + high * HD], preferred_element_type=jnp.float32
        )
        for b in range(low, high):
            here = slice((b - low) * HD, (b - low + 1) * HD)
            columns[b] = part[:, here] if columns[b] is None else jnp.where(inside[:, here], part[:, here], columns[b])
    enc_attn = jnp.concatenate(columns, axis=1).astype(jnp.bfloat16)
    res_third()
    loads[3].wait()
    collect(q_out, q_in, q_send, q_recv)
    width = new_kv.shape[1] // 2
    kv_heads = width // HD
    each = heads // kv_heads
    flip = (((1,), (1,)), ((), ()))
    scale = HD ** (-0.5) * LOG2E
    query = head_rows[...].astype(jnp.bfloat16)
    old = jnp.concatenate(
        [
            lax.dot_general(
                query[g * each:(g + 1) * each, :], cache[:, :, g * HD:(g + 1) * HD].reshape(-1, HD),
                flip, preferred_element_type=jnp.float32,
            )
            for g in range(kv_heads)
        ],
        axis=0,
    ) * scale
    token = lax.broadcasted_iota(jnp.int32, old.shape, 1)
    cached = token // TILE_LEN < jnp.broadcast_to(count_own[0], token.shape)
    old = jnp.where(cached, old, -jnp.inf)
    old_top = jnp.max(old, axis=-1, keepdims=True)
    old = jnp.where(cached, jnp.exp2(old - old_top), 0.0)
    old_total = jnp.sum(old, axis=-1, keepdims=True)
    old = old.astype(jnp.bfloat16)
    old_attn = jnp.concatenate(
        [
            jnp.dot(
                old[g * each:(g + 1) * each, :], cache[:, :, width + g * HD:width + (g + 1) * HD].reshape(-1, HD),
                preferred_element_type=jnp.float32,
            )
            for g in range(kv_heads)
        ],
        axis=0,
    )
    res_last()
    loads[1].wait()
    resid = own_tile(res_all, slice(0, res_own.shape[1])) + jnp.dot(
        enc_attn, weo[...], preferred_element_type=jnp.float32
    )
    features = layer_norm(resid).astype(jnp.bfloat16)

    loads[2].wait()
    new_kv[...] = jnp.dot(features, wkv[...], preferred_element_type=jnp.float32).astype(jnp.bfloat16)
    new = jnp.concatenate(
        [
            lax.dot_general(
                query[g * each:(g + 1) * each, :], new_kv[:, g * HD:(g + 1) * HD],
                flip, preferred_element_type=jnp.float32,
            )
            for g in range(kv_heads)
        ],
        axis=0,
    ) * scale
    top = jnp.maximum(old_top, jnp.max(new, axis=-1, keepdims=True))
    new = jnp.exp2(new - top)
    keep = jnp.exp2(old_top - top)
    share = 1.0 / (jnp.sum(new, axis=-1, keepdims=True) + old_total * keep)
    new = (new * share).astype(jnp.bfloat16)
    new_attn = jnp.concatenate(
        [
            jnp.dot(
                new[g * each:(g + 1) * each, :], new_kv[:, width + g * HD:width + (g + 1) * HD],
                preferred_element_type=jnp.float32,
            )
            for g in range(kv_heads)
        ],
        axis=0,
    )
    dec_attn = (old_attn * (keep * share) + new_attn).astype(jnp.bfloat16)
    attn_own[...] = dec_attn
    attn_all[me] = dec_attn
    widen(attn_all, me)
    attn_first, attn_second, attn_third, attn_fourth, attn_last, attn_drain = gather(
        attn_own, attn_all, attn_send, attn_recv, False, widen
    )
    attn_first()
    attn_second()
    attn_third()
    attn_fourth()
    attn_last()
    loads[4].wait()
    scatter(project(wo), o_out, o_in, o_send, o_recv)
    norm_drain()
    enc_drain()
    res_drain()
    attn_drain()
    collect(o_out, o_in, o_send, o_recv)
    result = (x_rows[...] + head_rows[...]).astype(jnp.bfloat16)
    for k in range(heads):
        out_ref[:, k * HD:(k + 1) * HD] = result[k:k + 1, :]


def fused(n, enc_x, enc_qkv, w_eo, w_kv, dec_x, w_q, w_o, cache_kv, doc_tile, cached_count):
    tok_rows = enc_x.shape[0]
    packed = (tok_rows, enc_qkv.shape[1] * enc_qkv.shape[2])
    heads = dec_x.shape[1] // HD
    tokens = n * tok_rows
    bf16, f32 = jnp.bfloat16, jnp.float32
    vmem = pl.BlockSpec(memory_space=pltpu.VMEM)
    hbm = pl.BlockSpec(memory_space=pl.ANY)
    dma = pltpu.SemaphoreType.DMA
    marks = n // 2
    piece = [pltpu.VMEM((heads, HD), bf16), pltpu.VMEM((n, heads, HD), bf16), dma((1,)), dma((marks,))]
    trade = [pltpu.VMEM((n, 2, HD), f32), pltpu.VMEM((n, 2, HD), f32), dma((1,)), dma((1,))]
    return pl.pallas_call(
        functools.partial(fused_kernel, n),
        out_shape=pltpu.VMEM(dec_x.shape, bf16),
        in_specs=[hbm] * 10,
        out_specs=vmem,
        scratch_shapes=[
            pltpu.VMEM(w_eo.shape, bf16),
            pltpu.VMEM(w_kv.shape, bf16),
            pltpu.VMEM(w_q.shape, bf16),
            pltpu.VMEM(w_o.shape, bf16),
            pltpu.VMEM(cache_kv.shape[1:], bf16),
            dma((12,)),
            pltpu.VMEM(dec_x.shape, bf16),
            pltpu.SMEM((1,), jnp.int32),
            pltpu.SMEM((1,), jnp.int32),
            pltpu.VMEM(packed, bf16),
            pltpu.VMEM((n,) + packed, bf16),
            dma((1,)),
            dma((marks,)),
            pltpu.VMEM(enc_x.shape, bf16),
            pltpu.VMEM((n,) + enc_x.shape, bf16),
            dma((1,)),
            dma((7,)),
            pltpu.VMEM((tokens, 2 * enc_qkv.shape[2]), bf16),
            pltpu.VMEM((TILE_LEN, w_kv.shape[1]), bf16),
            pltpu.VMEM((heads, HD), f32),
            *piece,
            *piece,
            pltpu.VMEM((n * (heads + 8), HD), f32),
            pltpu.VMEM((heads, HD), f32),
            *trade,
            *trade,
        ],
        compiler_params=pltpu.CompilerParams(collective_id=0, has_side_effects=True),
    )(enc_qkv.transpose(1, 0, 2), enc_x, dec_x, doc_tile, cached_count, w_eo, w_kv, w_q, w_o, cache_kv[0])

def solution(mesh):
    n = mesh.shape["seq"]
    return jax.shard_map(
        functools.partial(fused, n) if n == 32 else local,
        mesh=mesh,
        in_specs=(
            P(("group", "seq"), None),
            P(("group", "seq"), None, None),
            P(),
            P(),
            P(("group", "seq"), None),
            P(None, "seq"),
            P(None, "seq"),
            P(("group", "seq"), None, None, None),
            P(("group", "seq")),
            P(("group", "seq")),
        ),
        out_specs=P(("group", "seq"), None),
        check_vma=False,
    )
```

```python
import functools

import jax
import jax.numpy as jnp
from jax import lax
from jax.experimental import pallas as pl
from jax.experimental.pallas import tpu as pltpu
from jax.sharding import PartitionSpec as P

EH = 8
EHD = 80
HD = 128
TILE_LEN = 128
MESH = pl.DeviceIdType.MESH
LOG2E = 1.4426950408889634


def layer_norm(values):
    center = values - jnp.mean(values, axis=-1, keepdims=True)
    spread = jnp.mean(center * center, axis=-1, keepdims=True)
    return center * lax.rsqrt(spread + 1e-05)


def doc_attend(query_row, doc_kv, filled):
    length = doc_kv.shape[0]
    width = doc_kv.shape[1] // 2
    kv_heads = width // HD
    query_heads = query_row.reshape(kv_heads, -1, HD)
    key_heads = doc_kv[:, :width].reshape(length, kv_heads, HD)
    value_heads = doc_kv[:, width:].reshape(length, kv_heads, HD)
    scores = jnp.einsum(
        "gqd,kgd->gqk", query_heads, key_heads, preferred_element_type=jnp.float32
    ) * HD ** (-0.5)
    inside = jnp.arange(length, dtype=jnp.int32) // TILE_LEN <= filled
    scores = jnp.where(inside[None, None, :], scores, -jnp.inf)
    weights = jax.nn.softmax(scores, axis=-1).astype(jnp.bfloat16)
    result = jnp.einsum("gqk,kgd->gqd", weights, value_heads, preferred_element_type=jnp.float32)
    return result.reshape(1, -1).astype(jnp.bfloat16)


def local(enc_x, enc_qkv, w_eo, w_kv, dec_x, w_q, w_o, cache_kv, doc_tile, cached_count):
    tok_rows = enc_x.shape[0]
    query_heads = enc_qkv[:, 0].reshape(tok_rows, EH, EHD)
    key_piece = lax.all_gather(enc_qkv[:, 1], "seq", axis=0, tiled=True)
    value_piece = lax.all_gather(enc_qkv[:, 2], "seq", axis=0, tiled=True)
    length = key_piece.shape[0]
    key_heads = key_piece.reshape(length, EH, EHD)
    value_heads = value_piece.reshape(length, EH, EHD)
    scores = jnp.einsum(
        "qhd,khd->hqk", query_heads, key_heads, preferred_element_type=jnp.float32
    ) * EHD ** (-0.5)
    old_max = jnp.full((EH, tok_rows), -1e30, jnp.float32)
    new_max = jnp.maximum(old_max, jnp.max(scores, axis=-1))
    powers = jnp.exp(scores - new_max[:, :, None])
    new_total = jnp.sum(powers, axis=-1)
    new_acc = jnp.einsum(
        "hqk,khd->hqd", powers.astype(jnp.bfloat16), value_heads, preferred_element_type=jnp.float32
    )
    enc_attn = (
        (new_acc / new_total[:, :, None])
        .transpose(1, 0, 2)
        .reshape(tok_rows, -1)
        .astype(jnp.bfloat16)
    )
    resid = enc_x.astype(jnp.float32) + jnp.dot(enc_attn, w_eo, preferred_element_type=jnp.float32)
    features = layer_norm(resid).astype(jnp.bfloat16)
    tile_start = doc_tile[0] * TILE_LEN
    x_float = dec_x.astype(jnp.float32)
    normed = (
        x_float * lax.rsqrt(jnp.mean(x_float * x_float, axis=-1, keepdims=True) + 1e-05)
    ).astype(jnp.bfloat16)
    query_cols = jnp.dot(
        lax.all_gather(normed, "seq", axis=0, tiled=True), w_q, preferred_element_type=jnp.float32
    ).astype(jnp.bfloat16)
    query_row = lax.all_to_all(query_cols, "seq", split_axis=0, concat_axis=1, tiled=True)
    zero = jnp.zeros((), jnp.int32)
    filled = cached_count[0]
    local_kv = jnp.dot(features, w_kv, preferred_element_type=jnp.float32).astype(jnp.bfloat16)
    buffer = jnp.zeros((TILE_LEN, w_kv.shape[1]), jnp.bfloat16)
    piece = lax.all_gather(local_kv, "seq", axis=0, tiled=True)
    length = piece.shape[0]
    position = jnp.arange(length, dtype=jnp.int32) - tile_start
    inside = (position >= 0) & (position < buffer.shape[0])
    clipped = jnp.clip(position, 0, buffer.shape[0] - 1)
    tile_kv = buffer.at[clipped].add(jnp.where(inside[:, None], piece, jnp.zeros_like(piece)))
    doc_kv = lax.dynamic_update_slice(cache_kv[0], tile_kv[None], (filled, zero, zero))
    doc_kv = doc_kv.reshape(-1, doc_kv.shape[-1])
    dec_attn = doc_attend(query_row[0], doc_kv, filled)
    output_cols = jnp.dot(
        lax.all_gather(dec_attn, "seq", axis=0, tiled=True), w_o, preferred_element_type=jnp.float32
    ).astype(jnp.bfloat16)
    attn_out = lax.all_to_all(output_cols, "seq", split_axis=0, concat_axis=1, tiled=True)
    return (x_float + attn_out.astype(jnp.float32)).astype(jnp.bfloat16)


def fused_kernel(
    n, qkv_hbm, resid_hbm, x_hbm, tile_hbm, count_hbm, weo_hbm, wkv_hbm, wq_hbm, wo_hbm, cache_hbm, out_ref,
    weo, wkv, wq, wo, cache, load_sem, x_own, tile_own, count_own,
    enc_own, enc_all, enc_send, enc_recv, res_own, res_all, res_send, res_recv, mixed_ref, enc_rows, new_kv,
    x_rows, norm_own, norm_all, norm_send, norm_recv,
    attn_own, attn_all,
    wide, head_rows,
    q_out, q_in, q_send, q_recv,
    o_out, o_in,
):
    me = lax.axis_index("seq")
    inner = 4
    outer = n // (2 * inner)
    zi, qi, ci = me // (2 * inner), (me // 2) % inner, me % 2

    def at(kz, kq, kc):
        return (zi + kz) % outer * (2 * inner) + (qi + kq) % inner * 2 + (ci + kc) % 2

    barrier = pltpu.get_barrier_semaphore()

    partners = [at(kz, 0, 0) for kz in range(1, outer)] + [at(0, kq, 0) for kq in range(1, inner)] + [at(0, 0, 1)]
    for partner in partners:
        pl.semaphore_signal(barrier, inc=1, device_id={"seq": partner}, device_id_type=MESH)

    wide_a = EH * EHD
    heads = x_rows.shape[0]
    pitch = wide.shape[0] // n

    def widen(every, slot):
        wide[pl.ds(pl.multiple_of(slot * pitch, 8), heads), :] = every[slot].astype(jnp.float32)

    small = [
        pltpu.make_async_copy(src, dst, load_sem.at[5 + i])
        for i, (src, dst) in enumerate(
            [(x_hbm, x_own)]
            + [(qkv_hbm.at[j], enc_own.at[:, pl.ds(j * wide_a, wide_a)]) for j in range(3)]
            + [(resid_hbm, res_own)]
            + [(tile_hbm, tile_own), (count_hbm, count_own)]
        )
    ]
    for load in small:
        load.start()
    loads = [
        pltpu.make_async_copy(src, dst, load_sem.at[i])
        for i, (src, dst) in enumerate(
            ((wq_hbm, wq), (weo_hbm, weo), (wkv_hbm, wkv), (cache_hbm, cache), (wo_hbm, wo))
        )
    ]
    for load in loads:
        load.start()

    small[0].wait()
    for k in range(heads):
        x_rows[k:k + 1, :] = x_own[:, k * HD:(k + 1) * HD].astype(jnp.float32)
    x_float = x_rows[...]
    squares = jnp.sum(jnp.sum(x_float * x_float, axis=1, keepdims=True), axis=0, keepdims=True)
    normed = (x_float * lax.rsqrt(squares / x_float.size + 1e-05)).astype(jnp.bfloat16)
    norm_own[...] = normed
    norm_all[me] = normed
    widen(norm_all, me)
    for load in small[1:]:
        load.wait()
    enc_all[me] = enc_own[...]
    res_all[me] = res_own[...]
    pl.semaphore_wait(barrier, len(partners))

    flip_x = qi + 1 - 2 * (qi % 2)
    flip_y = (qi + 2) % inner
    flip_both = (flip_x + 2) % inner

    def place(kz, plane, core):
        return (zi + kz + outer) % outer * (2 * inner) + plane * 2 + core

    def gather(own, every, send, recv, merged, ready):
        each = 1 if merged else outer
        near, side, far, core = 0, (outer - 1, outer - 1 + each), outer - 1 + 2 * each, outer - 1 + 3 * each

        def nth(kz):
            return 0 if merged else kz

        def copy(src, slot, mark, device):
            return pltpu.make_async_remote_copy(
                src_ref=src, dst_ref=every.at[slot], send_sem=send.at[0], recv_sem=recv.at[mark],
                device_id={"seq": device}, device_id_type=MESH,
            )

        def push(src, slot, mark, device):
            copy(src, slot, mark, device).start()

        def take(slot, mark):
            copy(own, slot, mark, place(0, qi, 1 - ci)).wait_recv()

        def spread(src, slot, kz):
            push(src, slot, far + nth(kz), place(0, flip_both, ci))
            push(src, slot, side[0] + nth(kz), place(0, flip_x, ci))
            push(src, slot, side[1] + nth(kz), place(0, flip_y, ci))
            push(src, slot, core, place(0, qi, 1 - ci))

        def first(along=True, across=True):
            if along:
                for kz in range(1, outer):
                    push(own, me, near + kz - 1, place(kz, qi, ci))
            if across:
                spread(own, me, 0)

        def second(steps=range(1, outer)):
            for kz in steps:
                slot = place(-kz, qi, ci)
                take(slot, near + kz - 1)
                spread(every.at[slot], slot, kz)
                ready(every, slot)

        def pass_on(kz, plane, mark):
            slot = place(-kz, plane, ci)
            if not merged:
                take(slot, mark + kz)
            elif kz == 0:
                copy(every.at[pl.ds(0, outer)], pl.ds(0, outer), mark, place(0, qi, 1 - ci)).wait_recv()
            push(every.at[slot], slot, core, place(0, qi, 1 - ci))
            ready(every, slot)

        def third():
            for kz in range(outer):
                for odd, plane in enumerate((flip_x, flip_y)):
                    pass_on(kz, plane, side[odd])

        def fourth():
            for kz in range(outer):
                pass_on(kz, flip_both, far)

        def last():
            half = every.at[pl.ds(0, n // 2)]
            copy(half, pl.ds(0, n // 2), core, place(0, qi, 1 - ci)).wait_recv()
            for pair in range(n // 2):
                ready(every, 2 * pair + 1 - ci)

        def drain():
            most = every.at[pl.ds(0, n - 1)]
            copy(most, pl.ds(0, n - 1), core, place(0, qi, 1 - ci)).wait_send()

        return first, second, third, fourth, last, drain

    def scatter(values, out, into, send, recv):
        rounded = values.astype(jnp.bfloat16).astype(jnp.float32)
        for d in range(n):
            for half in range(2):
                out[d, half:half + 1, :] = rounded[d:d + 1, half * HD:(half + 1) * HD]

        def one(k, carry):
            device = (me + k) % n
            pltpu.make_async_remote_copy(
                src_ref=out.at[device], dst_ref=into.at[pl.ds(pl.multiple_of(2 * me, 2), 2)], send_sem=send.at[0], recv_sem=recv.at[0],
                device_id={"seq": device}, device_id_type=MESH,
            ).start()
            return carry

        lax.fori_loop(1, n, one, 0)
        into[pl.ds(2 * me, 2), :] = out[me]

    def collect(out, into, send, recv):
        copy = pltpu.make_async_remote_copy(
            src_ref=out.at[pl.ds(0, n - 1)], dst_ref=out.at[pl.ds(0, n - 1)], send_sem=send.at[0], recv_sem=recv.at[0],
            device_id={"seq": place(0, qi, 1 - ci)}, device_id_type=MESH,
        )
        copy.wait_recv()
        copy.wait_send()
        head_rows[...] = into[...]

    def project(weight):
        total = [None, None]
        for k in range(0, heads, 2):
            pair = [wide[pl.ds(k + j, n, stride=pitch), :] for j in range(2)]
            rows = jnp.concatenate(pair, axis=1).astype(jnp.bfloat16)
            for j in range(2):
                term = jnp.dot(
                    rows, weight[k * HD:(k + 2) * HD, j * HD:(j + 1) * HD], preferred_element_type=jnp.float32
                )
                total[j] = term if total[j] is None else total[j] + term
        return jnp.concatenate(total, axis=1)

    norm_first, norm_second, norm_third, norm_fourth, norm_last, norm_drain = gather(
        norm_own, norm_all, norm_send, norm_recv, False, widen
    )
    enc_first, enc_second, enc_third, enc_fourth, enc_last, enc_drain = gather(
        enc_own, enc_all, enc_send, enc_recv, True, lambda every, slot: None
    )
    def plane_gather(own, every, send, recv):
        core, along = inner - 1, inner
        across = (flip_x, flip_y, flip_both)

        def copy(src, to, mark, device):
            return pltpu.make_async_remote_copy(
                src_ref=src, dst_ref=every.at[to], send_sem=send.at[0], recv_sem=recv.at[mark],
                device_id={"seq": device}, device_id_type=MESH,
            )

        def several(count):
            return every.at[pl.ds(0, count)], pl.ds(0, count)

        def first():
            for mark, plane in enumerate(across):
                copy(own, me, mark, place(0, plane, ci)).start()
            copy(own, me, core, place(0, qi, 1 - ci)).start()

        def second():
            for mark, plane in enumerate(across):
                copy(own, place(0, plane, ci), mark, place(0, plane, ci)).wait_recv()
            for kz in range(1, outer):
                copy(own, me, along + kz - 1, place(kz, qi, ci)).start()
            for plane in across:
                slot = place(0, plane, ci)
                for kz in range(1, outer):
                    copy(every.at[slot], slot, along + kz - 1, place(kz, qi, ci)).start()
            for plane in across:
                slot = place(0, plane, ci)
                copy(every.at[slot], slot, core, place(0, qi, 1 - ci)).start()

        def third():
            for kz in range(1, outer):
                copy(*several(inner), along + kz - 1, place(kz, qi, ci)).wait_recv()
                for plane in (qi,) + across:
                    slot = place(-kz, plane, ci)
                    copy(every.at[slot], slot, core, place(0, qi, 1 - ci)).start()

        def last():
            copy(*several(n // 2), core, place(0, qi, 1 - ci)).wait_recv()

        def drain():
            copy(*several(n - 1), core, place(0, qi, 1 - ci)).wait_send()

        return first, second, third, last, drain

    res_first, res_second, res_third, res_last, res_drain = plane_gather(res_own, res_all, res_send, res_recv)
    norm_first()
    enc_first()
    res_first()
    norm_second()
    res_second()
    enc_second()
    norm_third()
    norm_fourth()
    norm_last()
    loads[0].wait()
    scatter(project(wq), q_out, q_in, q_send, q_recv)
    enc_third()
    enc_fourth()
    enc_last()

    tok_rows = enc_own.shape[0]
    group = 32 // tok_rows

    def unpack(j, carry):
        block = enc_all[pl.ds(j * group, group), :, wide_a:3 * wide_a].astype(jnp.float32)
        enc_rows[pl.ds(pl.multiple_of(j * 32, 32), 32), :] = block.reshape(32, -1).astype(jnp.bfloat16)
        return carry

    lax.fori_loop(0, n // group, unpack, 0)
    each_tile = TILE_LEN // tok_rows

    def own_tile(every, cols):
        rows = None
        for t in range(n // each_tile):
            there = every[t * each_tile:(t + 1) * each_tile, :, cols].astype(jnp.float32)
            there = there.reshape(TILE_LEN, -1)
            if rows is None:
                rows, chosen = there, jnp.broadcast_to(tile_own[0], there.shape)
            else:
                rows = jnp.where(chosen == t, there, rows)
        return rows

    queries = own_tile(enc_all, slice(0, wide_a)).astype(jnp.bfloat16)
    columns = [None] * (wide_a // HD)
    scored = []
    for h in range(EH):
        low, high = h * EHD // HD, (h * EHD + EHD - 1) // HD + 1
        span = slice(low * HD, high * HD)
        lane = lax.broadcasted_iota(jnp.int32, (1, (high - low) * HD), 1) + low * HD
        inside = (lane >= h * EHD) & (lane < (h + 1) * EHD)
        picked = jnp.where(inside, queries[:, span], jnp.zeros((), jnp.bfloat16))
        scores = lax.dot_general(
            picked, enc_rows[:, span], (((1,), (1,)), ((), ())), preferred_element_type=jnp.float32
        )
        scored.append((low, high, inside, scores))
    for low, high, inside, scores in scored:
        powers = jnp.exp2((scores - jnp.max(scores, axis=-1, keepdims=True)) * (EHD ** (-0.5) * LOG2E))
        weights = (powers * (1.0 / jnp.sum(powers, axis=-1, keepdims=True))).astype(jnp.bfloat16)
        part = jnp.dot(
            weights, enc_rows[:, wide_a + low * HD:wide_a + high * HD], preferred_element_type=jnp.float32
        )
        for b in range(low, high):
            here = slice((b - low) * HD, (b - low + 1) * HD)
            columns[b] = part[:, here] if columns[b] is None else jnp.where(inside[:, here], part[:, here], columns[b])
    enc_attn = jnp.concatenate(columns, axis=1).astype(jnp.bfloat16)
    loads[1].wait()
    mixed_ref[...] = jnp.dot(enc_attn, weo[...], preferred_element_type=jnp.float32)
    res_third()
    loads[3].wait()
    collect(q_out, q_in, q_send, q_recv)
    width = new_kv.shape[1] // 2
    kv_heads = width // HD
    each = heads // kv_heads
    flip = (((1,), (1,)), ((), ()))
    scale = HD ** (-0.5) * LOG2E
    query = head_rows[...].astype(jnp.bfloat16)
    old = jnp.concatenate(
        [
            lax.dot_general(
                query[g * each:(g + 1) * each, :], cache[:, :, g * HD:(g + 1) * HD].reshape(-1, HD),
                flip, preferred_element_type=jnp.float32,
            )
            for g in range(kv_heads)
        ],
        axis=0,
    ) * scale
    token = lax.broadcasted_iota(jnp.int32, old.shape, 1)
    cached = token // TILE_LEN < jnp.broadcast_to(count_own[0], token.shape)
    old = jnp.where(cached, old, -jnp.inf)
    old_top = jnp.max(old, axis=-1, keepdims=True)
    old = jnp.where(cached, jnp.exp2(old - old_top), 0.0)
    old_total = jnp.sum(old, axis=-1, keepdims=True)
    old = old.astype(jnp.bfloat16)
    old_attn = jnp.concatenate(
        [
            jnp.dot(
                old[g * each:(g + 1) * each, :], cache[:, :, width + g * HD:width + (g + 1) * HD].reshape(-1, HD),
                preferred_element_type=jnp.float32,
            )
            for g in range(kv_heads)
        ],
        axis=0,
    )
    res_last()
    resid = own_tile(res_all, slice(0, res_own.shape[1])) + mixed_ref[...]
    features = layer_norm(resid).astype(jnp.bfloat16)

    loads[2].wait()
    new_kv[...] = jnp.dot(features, wkv[...], preferred_element_type=jnp.float32).astype(jnp.bfloat16)
    new = jnp.concatenate(
        [
            lax.dot_general(
                query[g * each:(g + 1) * each, :], new_kv[:, g * HD:(g + 1) * HD],
                flip, preferred_element_type=jnp.float32,
            )
            for g in range(kv_heads)
        ],
        axis=0,
    ) * scale
    top = jnp.maximum(old_top, jnp.max(new, axis=-1, keepdims=True))
    new = jnp.exp2(new - top)
    keep = jnp.exp2(old_top - top)
    share = 1.0 / (jnp.sum(new, axis=-1, keepdims=True) + old_total * keep)
    new = (new * share).astype(jnp.bfloat16)
    new_attn = jnp.concatenate(
        [
            jnp.dot(
                new[g * each:(g + 1) * each, :], new_kv[:, width + g * HD:width + (g + 1) * HD],
                preferred_element_type=jnp.float32,
            )
            for g in range(kv_heads)
        ],
        axis=0,
    )
    dec_attn = (old_attn * (keep * share) + new_attn).astype(jnp.bfloat16)
    norm_drain()
    attn_own[...] = dec_attn
    attn_all[me] = dec_attn
    widen(attn_all, me)
    attn_first, attn_second, attn_third, attn_fourth, attn_last, attn_drain = gather(
        attn_own, attn_all, norm_send, norm_recv, False, widen
    )
    attn_first()
    attn_second()
    attn_third()
    attn_fourth()
    attn_last()
    loads[4].wait()
    scatter(project(wo), o_out, o_in, q_send, q_recv)
    enc_drain()
    res_drain()
    attn_drain()
    collect(o_out, o_in, q_send, q_recv)
    result = (x_rows[...] + head_rows[...]).astype(jnp.bfloat16)
    for k in range(heads):
        out_ref[:, k * HD:(k + 1) * HD] = result[k:k + 1, :]


def fused(n, enc_x, enc_qkv, w_eo, w_kv, dec_x, w_q, w_o, cache_kv, doc_tile, cached_count):
    tok_rows = enc_x.shape[0]
    packed = (tok_rows, enc_qkv.shape[1] * enc_qkv.shape[2])
    heads = dec_x.shape[1] // HD
    tokens = n * tok_rows
    bf16, f32 = jnp.bfloat16, jnp.float32
    vmem = pl.BlockSpec(memory_space=pltpu.VMEM)
    hbm = pl.BlockSpec(memory_space=pl.ANY)
    dma = pltpu.SemaphoreType.DMA
    marks = n // 2
    piece = [pltpu.VMEM((heads, HD), bf16), pltpu.VMEM((n, heads, HD), bf16), dma((1,)), dma((marks,))]
    trade = [pltpu.VMEM((n, 2, HD), f32), pltpu.VMEM((2 * n, HD), f32), dma((1,)), dma((1,))]
    return pl.pallas_call(
        functools.partial(fused_kernel, n),
        out_shape=pltpu.VMEM(dec_x.shape, bf16),
        in_specs=[hbm] * 10,
        out_specs=vmem,
        scratch_shapes=[
            pltpu.VMEM(w_eo.shape, bf16),
            pltpu.VMEM(w_kv.shape, bf16),
            pltpu.VMEM(w_q.shape, bf16),
            pltpu.VMEM(w_o.shape, bf16),
            pltpu.VMEM(cache_kv.shape[1:], bf16),
            dma((12,)),
            pltpu.VMEM(dec_x.shape, bf16),
            pltpu.SMEM((1,), jnp.int32),
            pltpu.SMEM((1,), jnp.int32),
            pltpu.VMEM(packed, bf16),
            pltpu.VMEM((n,) + packed, bf16),
            dma((1,)),
            dma((7,)),
            pltpu.VMEM(enc_x.shape, bf16),
            pltpu.VMEM((n,) + enc_x.shape, bf16),
            dma((1,)),
            dma((7,)),
            pltpu.VMEM((TILE_LEN, enc_x.shape[1]), f32),
            pltpu.VMEM((tokens, 2 * enc_qkv.shape[2]), bf16),
            pltpu.VMEM((TILE_LEN, w_kv.shape[1]), bf16),
            pltpu.VMEM((heads, HD), f32),
            *piece,
            *piece[:2],
            pltpu.VMEM((n * (heads + 8), HD), f32),
            pltpu.VMEM((heads, HD), f32),
            *trade,
            *trade[:2],
        ],
        compiler_params=pltpu.CompilerParams(collective_id=0, has_side_effects=True),
    )(enc_qkv.transpose(1, 0, 2), enc_x, dec_x, doc_tile, cached_count, w_eo, w_kv, w_q, w_o, cache_kv[0])

def solution(mesh):
    n = mesh.shape["seq"]
    return jax.shard_map(
        functools.partial(fused, n) if n == 32 else local,
        mesh=mesh,
        in_specs=(
            P(("group", "seq"), None),
            P(("group", "seq"), None, None),
            P(),
            P(),
            P(("group", "seq"), None),
            P(None, "seq"),
            P(None, "seq"),
            P(("group", "seq"), None, None, None),
            P(("group", "seq")),
            P(("group", "seq")),
        ),
        out_specs=P(("group", "seq"), None),
        check_vma=False,
    )
```

```python
import functools

import jax
import jax.numpy as jnp
from jax import lax
from jax.experimental import pallas as pl
from jax.experimental.pallas import tpu as pltpu
from jax.sharding import PartitionSpec as P

EH = 8
EHD = 80
HD = 128
TILE_LEN = 128
MESH = pl.DeviceIdType.MESH
LOG2E = 1.4426950408889634


def layer_norm(values):
    center = values - jnp.mean(values, axis=-1, keepdims=True)
    spread = jnp.mean(center * center, axis=-1, keepdims=True)
    return center * lax.rsqrt(spread + 1e-05)


def doc_attend(query_row, doc_kv, filled):
    length = doc_kv.shape[0]
    width = doc_kv.shape[1] // 2
    kv_heads = width // HD
    query_heads = query_row.reshape(kv_heads, -1, HD)
    key_heads = doc_kv[:, :width].reshape(length, kv_heads, HD)
    value_heads = doc_kv[:, width:].reshape(length, kv_heads, HD)
    scores = jnp.einsum(
        "gqd,kgd->gqk", query_heads, key_heads, preferred_element_type=jnp.float32
    ) * HD ** (-0.5)
    inside = jnp.arange(length, dtype=jnp.int32) // TILE_LEN <= filled
    scores = jnp.where(inside[None, None, :], scores, -jnp.inf)
    weights = jax.nn.softmax(scores, axis=-1).astype(jnp.bfloat16)
    result = jnp.einsum("gqk,kgd->gqd", weights, value_heads, preferred_element_type=jnp.float32)
    return result.reshape(1, -1).astype(jnp.bfloat16)


def local(enc_x, enc_qkv, w_eo, w_kv, dec_x, w_q, w_o, cache_kv, doc_tile, cached_count):
    tok_rows = enc_x.shape[0]
    query_heads = enc_qkv[:, 0].reshape(tok_rows, EH, EHD)
    key_piece = lax.all_gather(enc_qkv[:, 1], "seq", axis=0, tiled=True)
    value_piece = lax.all_gather(enc_qkv[:, 2], "seq", axis=0, tiled=True)
    length = key_piece.shape[0]
    key_heads = key_piece.reshape(length, EH, EHD)
    value_heads = value_piece.reshape(length, EH, EHD)
    scores = jnp.einsum(
        "qhd,khd->hqk", query_heads, key_heads, preferred_element_type=jnp.float32
    ) * EHD ** (-0.5)
    old_max = jnp.full((EH, tok_rows), -1e30, jnp.float32)
    new_max = jnp.maximum(old_max, jnp.max(scores, axis=-1))
    powers = jnp.exp(scores - new_max[:, :, None])
    new_total = jnp.sum(powers, axis=-1)
    new_acc = jnp.einsum(
        "hqk,khd->hqd", powers.astype(jnp.bfloat16), value_heads, preferred_element_type=jnp.float32
    )
    enc_attn = (
        (new_acc / new_total[:, :, None])
        .transpose(1, 0, 2)
        .reshape(tok_rows, -1)
        .astype(jnp.bfloat16)
    )
    resid = enc_x.astype(jnp.float32) + jnp.dot(enc_attn, w_eo, preferred_element_type=jnp.float32)
    features = layer_norm(resid).astype(jnp.bfloat16)
    tile_start = doc_tile[0] * TILE_LEN
    x_float = dec_x.astype(jnp.float32)
    normed = (
        x_float * lax.rsqrt(jnp.mean(x_float * x_float, axis=-1, keepdims=True) + 1e-05)
    ).astype(jnp.bfloat16)
    query_cols = jnp.dot(
        lax.all_gather(normed, "seq", axis=0, tiled=True), w_q, preferred_element_type=jnp.float32
    ).astype(jnp.bfloat16)
    query_row = lax.all_to_all(query_cols, "seq", split_axis=0, concat_axis=1, tiled=True)
    zero = jnp.zeros((), jnp.int32)
    filled = cached_count[0]
    local_kv = jnp.dot(features, w_kv, preferred_element_type=jnp.float32).astype(jnp.bfloat16)
    buffer = jnp.zeros((TILE_LEN, w_kv.shape[1]), jnp.bfloat16)
    piece = lax.all_gather(local_kv, "seq", axis=0, tiled=True)
    length = piece.shape[0]
    position = jnp.arange(length, dtype=jnp.int32) - tile_start
    inside = (position >= 0) & (position < buffer.shape[0])
    clipped = jnp.clip(position, 0, buffer.shape[0] - 1)
    tile_kv = buffer.at[clipped].add(jnp.where(inside[:, None], piece, jnp.zeros_like(piece)))
    doc_kv = lax.dynamic_update_slice(cache_kv[0], tile_kv[None], (filled, zero, zero))
    doc_kv = doc_kv.reshape(-1, doc_kv.shape[-1])
    dec_attn = doc_attend(query_row[0], doc_kv, filled)
    output_cols = jnp.dot(
        lax.all_gather(dec_attn, "seq", axis=0, tiled=True), w_o, preferred_element_type=jnp.float32
    ).astype(jnp.bfloat16)
    attn_out = lax.all_to_all(output_cols, "seq", split_axis=0, concat_axis=1, tiled=True)
    return (x_float + attn_out.astype(jnp.float32)).astype(jnp.bfloat16)


def fused_kernel(
    n, qkv_hbm, resid_hbm, x_hbm, tile_hbm, count_hbm, weo_hbm, wkv_hbm, wq_hbm, wo_hbm, cache_hbm, out_ref,
    weo, wkv, wq, wo, cache, load_sem, x_own, tile_own, count_own,
    enc_own, enc_all, enc_send, enc_recv, res_own, res_all, res_send, res_recv, mixed_ref, enc_rows, new_kv,
    x_rows, norm_own, norm_all, norm_send, norm_recv,
    attn_own, attn_all,
    wide, head_rows,
    q_out, q_in, q_send, q_recv,
    o_out, o_in,
):
    me = lax.axis_index("seq")
    inner = 4
    outer = n // (2 * inner)
    zi, qi, ci = me // (2 * inner), (me // 2) % inner, me % 2

    def at(kz, kq, kc):
        return (zi + kz) % outer * (2 * inner) + (qi + kq) % inner * 2 + (ci + kc) % 2

    barrier = pltpu.get_barrier_semaphore()

    partners = [at(kz, 0, 0) for kz in range(1, outer)] + [at(0, kq, 0) for kq in range(1, inner)] + [at(0, 0, 1)]
    for partner in partners:
        pl.semaphore_signal(barrier, inc=1, device_id={"seq": partner}, device_id_type=MESH)

    wide_a = EH * EHD
    heads = x_rows.shape[0]
    pitch = wide.shape[0] // n

    def widen(every, slot):
        wide[pl.ds(pl.multiple_of(slot * pitch, 8), heads), :] = every[slot].astype(jnp.float32)

    small = [
        pltpu.make_async_copy(src, dst, load_sem.at[5 + i])
        for i, (src, dst) in enumerate(
            [(x_hbm, x_own)]
            + [(qkv_hbm.at[j], enc_own.at[:, pl.ds(j * wide_a, wide_a)]) for j in range(3)]
            + [(resid_hbm, res_own)]
            + [(tile_hbm, tile_own), (count_hbm, count_own)]
        )
    ]
    for load in small:
        load.start()
    loads = [
        pltpu.make_async_copy(src, dst, load_sem.at[i])
        for i, (src, dst) in enumerate(
            ((wq_hbm, wq), (weo_hbm, weo), (wkv_hbm, wkv), (cache_hbm, cache), (wo_hbm, wo))
        )
    ]
    for load in loads:
        load.start()

    small[0].wait()
    for k in range(heads):
        x_rows[k:k + 1, :] = x_own[:, k * HD:(k + 1) * HD].astype(jnp.float32)
    x_float = x_rows[...]
    squares = jnp.sum(jnp.sum(x_float * x_float, axis=1, keepdims=True), axis=0, keepdims=True)
    normed = (x_float * lax.rsqrt(squares / x_float.size + 1e-05)).astype(jnp.bfloat16)
    norm_own[...] = normed
    norm_all[me] = normed
    widen(norm_all, me)
    for load in small[1:]:
        load.wait()
    enc_all[me] = enc_own[...]
    res_all[me] = res_own[...]
    pl.semaphore_wait(barrier, len(partners))

    flip_x = qi + 1 - 2 * (qi % 2)
    flip_y = (qi + 2) % inner
    flip_both = (flip_x + 2) % inner

    def place(kz, plane, core):
        return (zi + kz + outer) % outer * (2 * inner) + plane * 2 + core

    def gather(own, every, send, recv, merged, ready):
        each = 1 if merged else outer
        near, side, far, core = 0, (outer - 1, outer - 1 + each), outer - 1 + 2 * each, outer - 1 + 3 * each

        def nth(kz):
            return 0 if merged else kz

        def copy(src, slot, mark, device):
            return pltpu.make_async_remote_copy(
                src_ref=src, dst_ref=every.at[slot], send_sem=send.at[0], recv_sem=recv.at[mark],
                device_id={"seq": device}, device_id_type=MESH,
            )

        def push(src, slot, mark, device):
            copy(src, slot, mark, device).start()

        def take(slot, mark):
            copy(own, slot, mark, place(0, qi, 1 - ci)).wait_recv()

        def spread(src, slot, kz):
            push(src, slot, far + nth(kz), place(0, flip_both, ci))
            push(src, slot, side[0] + nth(kz), place(0, flip_x, ci))
            push(src, slot, side[1] + nth(kz), place(0, flip_y, ci))
            push(src, slot, core, place(0, qi, 1 - ci))

        def first(along=True, across=True):
            if along:
                for kz in range(1, outer):
                    push(own, me, near + kz - 1, place(kz, qi, ci))
            if across:
                spread(own, me, 0)

        def second(steps=range(1, outer)):
            for kz in steps:
                slot = place(-kz, qi, ci)
                take(slot, near + kz - 1)
                spread(every.at[slot], slot, kz)
                ready(every, slot)

        def pass_on(kz, plane, mark):
            slot = place(-kz, plane, ci)
            if not merged:
                take(slot, mark + kz)
            elif kz == 0:
                copy(every.at[pl.ds(0, outer)], pl.ds(0, outer), mark, place(0, qi, 1 - ci)).wait_recv()
            push(every.at[slot], slot, core, place(0, qi, 1 - ci))
            ready(every, slot)

        def third():
            for kz in range(outer):
                for odd, plane in enumerate((flip_x, flip_y)):
                    pass_on(kz, plane, side[odd])

        def fourth():
            for kz in range(outer):
                pass_on(kz, flip_both, far)

        def last():
            half = every.at[pl.ds(0, n // 2)]
            copy(half, pl.ds(0, n // 2), core, place(0, qi, 1 - ci)).wait_recv()
            for pair in range(n // 2):
                ready(every, 2 * pair + 1 - ci)

        def drain():
            most = every.at[pl.ds(0, n - 1)]
            copy(most, pl.ds(0, n - 1), core, place(0, qi, 1 - ci)).wait_send()

        return first, second, third, fourth, last, drain

    def scatter(values, out, into, send, recv):
        rounded = values.astype(jnp.bfloat16).astype(jnp.float32)
        for d in range(n):
            for half in range(2):
                out[d, half:half + 1, :] = rounded[d:d + 1, half * HD:(half + 1) * HD]

        def one(k, carry):
            device = (me + k) % n
            pltpu.make_async_remote_copy(
                src_ref=out.at[device], dst_ref=into.at[pl.ds(pl.multiple_of(2 * me, 2), 2)], send_sem=send.at[0], recv_sem=recv.at[0],
                device_id={"seq": device}, device_id_type=MESH,
            ).start()
            return carry

        lax.fori_loop(1, n, one, 0, unroll=True)
        into[pl.ds(2 * me, 2), :] = out[me]

    def collect(out, into, send, recv):
        copy = pltpu.make_async_remote_copy(
            src_ref=out.at[pl.ds(0, n - 1)], dst_ref=out.at[pl.ds(0, n - 1)], send_sem=send.at[0], recv_sem=recv.at[0],
            device_id={"seq": place(0, qi, 1 - ci)}, device_id_type=MESH,
        )
        copy.wait_recv()
        copy.wait_send()
        head_rows[...] = into[...]

    def project(weight):
        total = [None, None]
        for k in range(0, heads, 2):
            pair = [wide[pl.ds(k + j, n, stride=pitch), :] for j in range(2)]
            rows = jnp.concatenate(pair, axis=1).astype(jnp.bfloat16)
            for j in range(2):
                term = jnp.dot(
                    rows, weight[k * HD:(k + 2) * HD, j * HD:(j + 1) * HD], preferred_element_type=jnp.float32
                )
                total[j] = term if total[j] is None else total[j] + term
        return jnp.concatenate(total, axis=1)

    norm_first, norm_second, norm_third, norm_fourth, norm_last, norm_drain = gather(
        norm_own, norm_all, norm_send, norm_recv, False, widen
    )
    enc_first, enc_second, enc_third, enc_fourth, enc_last, enc_drain = gather(
        enc_own, enc_all, enc_send, enc_recv, True, lambda every, slot: None
    )
    def plane_gather(own, every, send, recv):
        core, along = inner - 1, inner
        across = (flip_x, flip_y, flip_both)

        def copy(src, to, mark, device):
            return pltpu.make_async_remote_copy(
                src_ref=src, dst_ref=every.at[to], send_sem=send.at[0], recv_sem=recv.at[mark],
                device_id={"seq": device}, device_id_type=MESH,
            )

        def several(count):
            return every.at[pl.ds(0, count)], pl.ds(0, count)

        def first():
            for mark, plane in enumerate(across):
                copy(own, me, mark, place(0, plane, ci)).start()
            copy(own, me, core, place(0, qi, 1 - ci)).start()

        def second():
            for mark, plane in enumerate(across):
                copy(own, place(0, plane, ci), mark, place(0, plane, ci)).wait_recv()
            for kz in range(1, outer):
                copy(own, me, along + kz - 1, place(kz, qi, ci)).start()
            for plane in across:
                slot = place(0, plane, ci)
                for kz in range(1, outer):
                    copy(every.at[slot], slot, along + kz - 1, place(kz, qi, ci)).start()
            for plane in across:
                slot = place(0, plane, ci)
                copy(every.at[slot], slot, core, place(0, qi, 1 - ci)).start()

        def third():
            for kz in range(1, outer):
                copy(*several(inner), along + kz - 1, place(kz, qi, ci)).wait_recv()
                for plane in (qi,) + across:
                    slot = place(-kz, plane, ci)
                    copy(every.at[slot], slot, core, place(0, qi, 1 - ci)).start()

        def last():
            copy(*several(n // 2), core, place(0, qi, 1 - ci)).wait_recv()

        def drain():
            copy(*several(n - 1), core, place(0, qi, 1 - ci)).wait_send()

        return first, second, third, last, drain

    res_first, res_second, res_third, res_last, res_drain = plane_gather(res_own, res_all, res_send, res_recv)
    norm_first()
    enc_first()
    res_first()
    norm_second()
    enc_second((1,))
    res_second()
    enc_second((2,3))
    norm_third()
    norm_fourth()
    norm_last()
    loads[0].wait()
    scatter(project(wq), q_out, q_in, q_send, q_recv)
    enc_third()
    enc_fourth()
    enc_last()

    tok_rows = enc_own.shape[0]
    group = 32 // tok_rows

    def unpack(j, carry):
        block = enc_all[pl.ds(j * group, group), :, wide_a:3 * wide_a].astype(jnp.float32)
        enc_rows[pl.ds(pl.multiple_of(j * 32, 32), 32), :] = block.reshape(32, -1).astype(jnp.bfloat16)
        return carry

    lax.fori_loop(0, n // group, unpack, 0)
    each_tile = TILE_LEN // tok_rows

    def own_tile(every, cols):
        rows = None
        for t in range(n // each_tile):
            there = every[t * each_tile:(t + 1) * each_tile, :, cols].astype(jnp.float32)
            there = there.reshape(TILE_LEN, -1)
            if rows is None:
                rows, chosen = there, jnp.broadcast_to(tile_own[0], there.shape)
            else:
                rows = jnp.where(chosen == t, there, rows)
        return rows

    queries = own_tile(enc_all, slice(0, wide_a)).astype(jnp.bfloat16)
    columns = [None] * (wide_a // HD)
    scored = []
    for h in range(EH):
        low, high = h * EHD // HD, (h * EHD + EHD - 1) // HD + 1
        span = slice(low * HD, high * HD)
        lane = lax.broadcasted_iota(jnp.int32, (1, (high - low) * HD), 1) + low * HD
        inside = (lane >= h * EHD) & (lane < (h + 1) * EHD)
        picked = jnp.where(inside, queries[:, span], jnp.zeros((), jnp.bfloat16))
        scores = lax.dot_general(
            picked, enc_rows[:, span], (((1,), (1,)), ((), ())), preferred_element_type=jnp.float32
        )
        scored.append((low, high, inside, scores))
    for low, high, inside, scores in scored:
        powers = jnp.exp2((scores - jnp.max(scores, axis=-1, keepdims=True)) * (EHD ** (-0.5) * LOG2E))
        weights = (powers * (1.0 / jnp.sum(powers, axis=-1, keepdims=True))).astype(jnp.bfloat16)
        part = jnp.dot(
            weights, enc_rows[:, wide_a + low * HD:wide_a + high * HD], preferred_element_type=jnp.float32
        )
        for b in range(low, high):
            here = slice((b - low) * HD, (b - low + 1) * HD)
            columns[b] = part[:, here] if columns[b] is None else jnp.where(inside[:, here], part[:, here], columns[b])
    enc_attn = jnp.concatenate(columns, axis=1).astype(jnp.bfloat16)
    loads[1].wait()
    mixed_ref[...] = jnp.dot(enc_attn, weo[...], preferred_element_type=jnp.float32)
    res_third()
    loads[3].wait()
    collect(q_out, q_in, q_send, q_recv)
    width = new_kv.shape[1] // 2
    kv_heads = width // HD
    each = heads // kv_heads
    flip = (((1,), (1,)), ((), ()))
    scale = HD ** (-0.5) * LOG2E
    query = head_rows[...].astype(jnp.bfloat16)
    old = jnp.concatenate(
        [
            lax.dot_general(
                query[g * each:(g + 1) * each, :], cache[:, :, g * HD:(g + 1) * HD].reshape(-1, HD),
                flip, preferred_element_type=jnp.float32,
            )
            for g in range(kv_heads)
        ],
        axis=0,
    ) * scale
    token = lax.broadcasted_iota(jnp.int32, old.shape, 1)
    cached = token // TILE_LEN < jnp.broadcast_to(count_own[0], token.shape)
    old = jnp.where(cached, old, -jnp.inf)
    old_top = jnp.max(old, axis=-1, keepdims=True)
    old = jnp.where(cached, jnp.exp2(old - old_top), 0.0)
    old_total = jnp.sum(old, axis=-1, keepdims=True)
    old = old.astype(jnp.bfloat16)
    old_attn = jnp.concatenate(
        [
            jnp.dot(
                old[g * each:(g + 1) * each, :], cache[:, :, width + g * HD:width + (g + 1) * HD].reshape(-1, HD),
                preferred_element_type=jnp.float32,
            )
            for g in range(kv_heads)
        ],
        axis=0,
    )
    res_last()
    resid = own_tile(res_all, slice(0, res_own.shape[1])) + mixed_ref[...]
    features = layer_norm(resid).astype(jnp.bfloat16)

    loads[2].wait()
    new_kv[...] = jnp.dot(features, wkv[...], preferred_element_type=jnp.float32).astype(jnp.bfloat16)
    new = jnp.concatenate(
        [
            lax.dot_general(
                query[g * each:(g + 1) * each, :], new_kv[:, g * HD:(g + 1) * HD],
                flip, preferred_element_type=jnp.float32,
            )
            for g in range(kv_heads)
        ],
        axis=0,
    ) * scale
    top = jnp.maximum(old_top, jnp.max(new, axis=-1, keepdims=True))
    new = jnp.exp2(new - top)
    keep = jnp.exp2(old_top - top)
    share = 1.0 / (jnp.sum(new, axis=-1, keepdims=True) + old_total * keep)
    new = (new * share).astype(jnp.bfloat16)
    new_attn = jnp.concatenate(
        [
            jnp.dot(
                new[g * each:(g + 1) * each, :], new_kv[:, width + g * HD:width + (g + 1) * HD],
                preferred_element_type=jnp.float32,
            )
            for g in range(kv_heads)
        ],
        axis=0,
    )
    dec_attn = (old_attn * (keep * share) + new_attn).astype(jnp.bfloat16)
    norm_drain()
    attn_own[...] = dec_attn
    attn_all[me] = dec_attn
    widen(attn_all, me)
    attn_first, attn_second, attn_third, attn_fourth, attn_last, attn_drain = gather(
        attn_own, attn_all, norm_send, norm_recv, False, widen
    )
    attn_first()
    attn_second()
    attn_third()
    attn_fourth()
    attn_last()
    loads[4].wait()
    scatter(project(wo), o_out, o_in, q_send, q_recv)
    enc_drain()
    res_drain()
    attn_drain()
    collect(o_out, o_in, q_send, q_recv)
    result = (x_rows[...] + head_rows[...]).astype(jnp.bfloat16)
    out_ref[...] = result.reshape(1, -1)


def fused(n, enc_x, enc_qkv, w_eo, w_kv, dec_x, w_q, w_o, cache_kv, doc_tile, cached_count):
    tok_rows = enc_x.shape[0]
    packed = (tok_rows, enc_qkv.shape[1] * enc_qkv.shape[2])
    heads = dec_x.shape[1] // HD
    tokens = n * tok_rows
    bf16, f32 = jnp.bfloat16, jnp.float32
    vmem = pl.BlockSpec(memory_space=pltpu.VMEM)
    hbm = pl.BlockSpec(memory_space=pl.ANY)
    dma = pltpu.SemaphoreType.DMA
    marks = n // 2
    piece = [pltpu.VMEM((heads, HD), bf16), pltpu.VMEM((n, heads, HD), bf16), dma((1,)), dma((marks,))]
    trade = [pltpu.VMEM((n, 2, HD), f32), pltpu.VMEM((2 * n, HD), f32), dma((1,)), dma((1,))]
    return pl.pallas_call(
        functools.partial(fused_kernel, n),
        out_shape=pltpu.VMEM(dec_x.shape, bf16),
        in_specs=[hbm] * 10,
        out_specs=vmem,
        scratch_shapes=[
            pltpu.VMEM(w_eo.shape, bf16),
            pltpu.VMEM(w_kv.shape, bf16),
            pltpu.VMEM(w_q.shape, bf16),
            pltpu.VMEM(w_o.shape, bf16),
            pltpu.VMEM(cache_kv.shape[1:], bf16),
            dma((12,)),
            pltpu.VMEM(dec_x.shape, bf16),
            pltpu.SMEM((1,), jnp.int32),
            pltpu.SMEM((1,), jnp.int32),
            pltpu.VMEM(packed, bf16),
            pltpu.VMEM((n,) + packed, bf16),
            dma((1,)),
            dma((7,)),
            pltpu.VMEM(enc_x.shape, bf16),
            pltpu.VMEM((n,) + enc_x.shape, bf16),
            dma((1,)),
            dma((7,)),
            pltpu.VMEM((TILE_LEN, enc_x.shape[1]), f32),
            pltpu.VMEM((tokens, 2 * enc_qkv.shape[2]), bf16),
            pltpu.VMEM((TILE_LEN, w_kv.shape[1]), bf16),
            pltpu.VMEM((heads, HD), f32),
            *piece,
            *piece[:2],
            pltpu.VMEM((n * (heads + 8), HD), f32),
            pltpu.VMEM((heads, HD), f32),
            *trade,
            *trade[:2],
        ],
        compiler_params=pltpu.CompilerParams(collective_id=0, has_side_effects=True),
    )(enc_qkv.transpose(1, 0, 2), enc_x, dec_x, doc_tile, cached_count, w_eo, w_kv, w_q, w_o, cache_kv[0])

def solution(mesh):
    n = mesh.shape["seq"]
    return jax.shard_map(
        functools.partial(fused, n) if n == 32 else local,
        mesh=mesh,
        in_specs=(
            P(("group", "seq"), None),
            P(("group", "seq"), None, None),
            P(),
            P(),
            P(("group", "seq"), None),
            P(None, "seq"),
            P(None, "seq"),
            P(("group", "seq"), None, None, None),
            P(("group", "seq")),
            P(("group", "seq")),
        ),
        out_specs=P(("group", "seq"), None),
        check_vma=False,
    )
```

```python
import functools

import jax
import jax.numpy as jnp
from jax import lax
from jax.experimental import pallas as pl
from jax.experimental.pallas import tpu as pltpu
from jax.sharding import PartitionSpec as P

EH = 8
EHD = 80
HD = 128
TILE_LEN = 128
MESH = pl.DeviceIdType.MESH
LOG2E = 1.4426950408889634


def layer_norm(values):
    center = values - jnp.mean(values, axis=-1, keepdims=True)
    spread = jnp.mean(center * center, axis=-1, keepdims=True)
    return center * lax.rsqrt(spread + 1e-05)


def doc_attend(query_row, doc_kv, filled):
    length = doc_kv.shape[0]
    width = doc_kv.shape[1] // 2
    kv_heads = width // HD
    query_heads = query_row.reshape(kv_heads, -1, HD)
    key_heads = doc_kv[:, :width].reshape(length, kv_heads, HD)
    value_heads = doc_kv[:, width:].reshape(length, kv_heads, HD)
    scores = jnp.einsum(
        "gqd,kgd->gqk", query_heads, key_heads, preferred_element_type=jnp.float32
    ) * HD ** (-0.5)
    inside = jnp.arange(length, dtype=jnp.int32) // TILE_LEN <= filled
    scores = jnp.where(inside[None, None, :], scores, -jnp.inf)
    weights = jax.nn.softmax(scores, axis=-1).astype(jnp.bfloat16)
    result = jnp.einsum("gqk,kgd->gqd", weights, value_heads, preferred_element_type=jnp.float32)
    return result.reshape(1, -1).astype(jnp.bfloat16)


def local(enc_x, enc_qkv, w_eo, w_kv, dec_x, w_q, w_o, cache_kv, doc_tile, cached_count):
    tok_rows = enc_x.shape[0]
    query_heads = enc_qkv[:, 0].reshape(tok_rows, EH, EHD)
    key_piece = lax.all_gather(enc_qkv[:, 1], "seq", axis=0, tiled=True)
    value_piece = lax.all_gather(enc_qkv[:, 2], "seq", axis=0, tiled=True)
    length = key_piece.shape[0]
    key_heads = key_piece.reshape(length, EH, EHD)
    value_heads = value_piece.reshape(length, EH, EHD)
    scores = jnp.einsum(
        "qhd,khd->hqk", query_heads, key_heads, preferred_element_type=jnp.float32
    ) * EHD ** (-0.5)
    old_max = jnp.full((EH, tok_rows), -1e30, jnp.float32)
    new_max = jnp.maximum(old_max, jnp.max(scores, axis=-1))
    powers = jnp.exp(scores - new_max[:, :, None])
    new_total = jnp.sum(powers, axis=-1)
    new_acc = jnp.einsum(
        "hqk,khd->hqd", powers.astype(jnp.bfloat16), value_heads, preferred_element_type=jnp.float32
    )
    enc_attn = (
        (new_acc / new_total[:, :, None])
        .transpose(1, 0, 2)
        .reshape(tok_rows, -1)
        .astype(jnp.bfloat16)
    )
    resid = enc_x.astype(jnp.float32) + jnp.dot(enc_attn, w_eo, preferred_element_type=jnp.float32)
    features = layer_norm(resid).astype(jnp.bfloat16)
    tile_start = doc_tile[0] * TILE_LEN
    x_float = dec_x.astype(jnp.float32)
    normed = (
        x_float * lax.rsqrt(jnp.mean(x_float * x_float, axis=-1, keepdims=True) + 1e-05)
    ).astype(jnp.bfloat16)
    query_cols = jnp.dot(
        lax.all_gather(normed, "seq", axis=0, tiled=True), w_q, preferred_element_type=jnp.float32
    ).astype(jnp.bfloat16)
    query_row = lax.all_to_all(query_cols, "seq", split_axis=0, concat_axis=1, tiled=True)
    zero = jnp.zeros((), jnp.int32)
    filled = cached_count[0]
    local_kv = jnp.dot(features, w_kv, preferred_element_type=jnp.float32).astype(jnp.bfloat16)
    buffer = jnp.zeros((TILE_LEN, w_kv.shape[1]), jnp.bfloat16)
    piece = lax.all_gather(local_kv, "seq", axis=0, tiled=True)
    length = piece.shape[0]
    position = jnp.arange(length, dtype=jnp.int32) - tile_start
    inside = (position >= 0) & (position < buffer.shape[0])
    clipped = jnp.clip(position, 0, buffer.shape[0] - 1)
    tile_kv = buffer.at[clipped].add(jnp.where(inside[:, None], piece, jnp.zeros_like(piece)))
    doc_kv = lax.dynamic_update_slice(cache_kv[0], tile_kv[None], (filled, zero, zero))
    doc_kv = doc_kv.reshape(-1, doc_kv.shape[-1])
    dec_attn = doc_attend(query_row[0], doc_kv, filled)
    output_cols = jnp.dot(
        lax.all_gather(dec_attn, "seq", axis=0, tiled=True), w_o, preferred_element_type=jnp.float32
    ).astype(jnp.bfloat16)
    attn_out = lax.all_to_all(output_cols, "seq", split_axis=0, concat_axis=1, tiled=True)
    return (x_float + attn_out.astype(jnp.float32)).astype(jnp.bfloat16)


def fused_kernel(
    n, qkv_hbm, resid_hbm, x_hbm, tile_hbm, count_hbm, weo_hbm, wkv_hbm, wq_hbm, wo_hbm, cache_hbm, out_ref,
    weo, wkv, wq, wo, cache, load_sem, x_own, tile_own, count_own,
    enc_own, enc_all, enc_send, enc_recv, res_own, res_all, res_send, res_recv, mixed_ref, enc_rows, new_kv,
    x_rows, norm_own, norm_all, norm_send, norm_recv,
    attn_own, attn_all,
    wide, head_rows,
    q_out, q_in, q_send, q_recv,
    o_out, o_in,
):
    me = lax.axis_index("seq")
    inner = 4
    outer = n // (2 * inner)
    zi, qi, ci = me // (2 * inner), (me // 2) % inner, me % 2

    def at(kz, kq, kc):
        return (zi + kz) % outer * (2 * inner) + (qi + kq) % inner * 2 + (ci + kc) % 2

    barrier = pltpu.get_barrier_semaphore()

    partners = [at(kz, 0, 0) for kz in range(1, outer)] + [at(0, kq, 0) for kq in range(1, inner)] + [at(0, 0, 1)]
    for partner in partners:
        pl.semaphore_signal(barrier, inc=1, device_id={"seq": partner}, device_id_type=MESH)

    wide_a = EH * EHD
    heads = x_rows.shape[0]
    pitch = wide.shape[0] // n

    def widen(every, slot):
        wide[pl.ds(pl.multiple_of(slot * pitch, 8), heads), :] = every[slot].astype(jnp.float32)

    small = [
        pltpu.make_async_copy(src, dst, load_sem.at[5 + i])
        for i, (src, dst) in enumerate(
            [(x_hbm, x_own)]
            + [(qkv_hbm.at[j], enc_own.at[:, pl.ds(j * wide_a, wide_a)]) for j in range(3)]
            + [(resid_hbm, res_own)]
            + [(tile_hbm, tile_own), (count_hbm, count_own)]
        )
    ]
    for load in small:
        load.start()
    loads = [
        pltpu.make_async_copy(src, dst, load_sem.at[i])
        for i, (src, dst) in enumerate(
            ((wq_hbm, wq), (weo_hbm, weo), (wkv_hbm, wkv), (cache_hbm, cache), (wo_hbm, wo))
        )
    ]
    for load in loads:
        load.start()

    small[0].wait()
    for k in range(heads):
        x_rows[k:k + 1, :] = x_own[:, k * HD:(k + 1) * HD].astype(jnp.float32)
    x_float = x_rows[...]
    squares = jnp.sum(jnp.sum(x_float * x_float, axis=1, keepdims=True), axis=0, keepdims=True)
    normed = (x_float * lax.rsqrt(squares / x_float.size + 1e-05)).astype(jnp.bfloat16)
    norm_own[...] = normed
    norm_all[me] = normed
    widen(norm_all, me)
    for load in small[1:]:
        load.wait()
    enc_all[me] = enc_own[...]
    res_all[me] = res_own[...]
    pl.semaphore_wait(barrier, len(partners))

    flip_x = qi + 1 - 2 * (qi % 2)
    flip_y = (qi + 2) % inner
    flip_both = (flip_x + 2) % inner

    def place(kz, plane, core):
        return (zi + kz + outer) % outer * (2 * inner) + plane * 2 + core

    def gather(own, every, send, recv, merged, ready):
        each = 1 if merged else outer
        near, side, far, core = 0, (outer - 1, outer - 1 + each), outer - 1 + 2 * each, outer - 1 + 3 * each

        def nth(kz):
            return 0 if merged else kz

        def copy(src, slot, mark, device):
            return pltpu.make_async_remote_copy(
                src_ref=src, dst_ref=every.at[slot], send_sem=send.at[0], recv_sem=recv.at[mark],
                device_id={"seq": device}, device_id_type=MESH,
            )

        def push(src, slot, mark, device):
            copy(src, slot, mark, device).start()

        def take(slot, mark):
            copy(own, slot, mark, place(0, qi, 1 - ci)).wait_recv()

        def spread(src, slot, kz):
            push(src, slot, far + nth(kz), place(0, flip_both, ci))
            push(src, slot, side[0] + nth(kz), place(0, flip_x, ci))
            push(src, slot, side[1] + nth(kz), place(0, flip_y, ci))
            push(src, slot, core, place(0, qi, 1 - ci))

        def first(along=True, across=True):
            if along:
                for kz in range(1, outer):
                    push(own, me, near + kz - 1, place(kz, qi, ci))
            if across:
                spread(own, me, 0)

        def second(steps=range(1, outer)):
            for kz in steps:
                slot = place(-kz, qi, ci)
                take(slot, near + kz - 1)
                spread(every.at[slot], slot, kz)
                ready(every, slot)

        def pass_on(kz, plane, mark):
            slot = place(-kz, plane, ci)
            if not merged:
                take(slot, mark + kz)
            elif kz == 0:
                copy(every.at[pl.ds(0, outer)], pl.ds(0, outer), mark, place(0, qi, 1 - ci)).wait_recv()
            push(every.at[slot], slot, core, place(0, qi, 1 - ci))
            ready(every, slot)

        def third():
            for kz in range(outer):
                for odd, plane in enumerate((flip_x, flip_y)):
                    pass_on(kz, plane, side[odd])

        def fourth():
            for kz in range(outer):
                pass_on(kz, flip_both, far)

        def last():
            half = every.at[pl.ds(0, n // 2)]
            copy(half, pl.ds(0, n // 2), core, place(0, qi, 1 - ci)).wait_recv()
            for pair in range(n // 2):
                ready(every, 2 * pair + 1 - ci)

        def drain():
            most = every.at[pl.ds(0, n - 1)]
            copy(most, pl.ds(0, n - 1), core, place(0, qi, 1 - ci)).wait_send()

        return first, second, third, fourth, last, drain

    def scatter(values, out, into, send, recv):
        rounded = values.astype(jnp.bfloat16).astype(jnp.float32)
        for d in range(n):
            for half in range(2):
                out[d, half:half + 1, :] = rounded[d:d + 1, half * HD:(half + 1) * HD]

        def one(k, carry):
            device = (me + k) % n
            pltpu.make_async_remote_copy(
                src_ref=out.at[device], dst_ref=into.at[pl.ds(pl.multiple_of(2 * me, 2), 2)], send_sem=send.at[0], recv_sem=recv.at[0],
                device_id={"seq": device}, device_id_type=MESH,
            ).start()
            return carry

        lax.fori_loop(1, n, one, 0, unroll=True)
        into[pl.ds(2 * me, 2), :] = out[me]

    def collect(out, into, send, recv):
        copy = pltpu.make_async_remote_copy(
            src_ref=out.at[pl.ds(0, n - 1)], dst_ref=out.at[pl.ds(0, n - 1)], send_sem=send.at[0], recv_sem=recv.at[0],
            device_id={"seq": place(0, qi, 1 - ci)}, device_id_type=MESH,
        )
        copy.wait_recv()
        copy.wait_send()
        head_rows[...] = into[...]

    def project(weight):
        total = [None, None]
        for k in range(0, heads, 2):
            pair = [wide[pl.ds(k + j, n, stride=pitch), :] for j in range(2)]
            rows = jnp.concatenate(pair, axis=1).astype(jnp.bfloat16)
            for j in range(2):
                term = jnp.dot(
                    rows, weight[k * HD:(k + 2) * HD, j * HD:(j + 1) * HD], preferred_element_type=jnp.float32
                )
                total[j] = term if total[j] is None else total[j] + term
        return jnp.concatenate(total, axis=1)

    norm_first, norm_second, norm_third, norm_fourth, norm_last, norm_drain = gather(
        norm_own, norm_all, norm_send, norm_recv, False, widen
    )
    enc_first, enc_second, enc_third, enc_fourth, enc_last, enc_drain = gather(
        enc_own, enc_all, enc_send, enc_recv, True, lambda every, slot: None
    )
    def plane_gather(own, every, send, recv):
        core, along = inner - 1, inner
        across = (flip_x, flip_y, flip_both)

        def copy(src, to, mark, device):
            return pltpu.make_async_remote_copy(
                src_ref=src, dst_ref=every.at[to], send_sem=send.at[0], recv_sem=recv.at[mark],
                device_id={"seq": device}, device_id_type=MESH,
            )

        def several(count):
            return every.at[pl.ds(0, count)], pl.ds(0, count)

        def first():
            for mark, plane in enumerate(across):
                copy(own, me, mark, place(0, plane, ci)).start()
            copy(own, me, core, place(0, qi, 1 - ci)).start()

        def second():
            for mark, plane in enumerate(across):
                copy(own, place(0, plane, ci), mark, place(0, plane, ci)).wait_recv()
            for kz in range(1, outer):
                copy(own, me, along + kz - 1, place(kz, qi, ci)).start()
            for plane in across:
                slot = place(0, plane, ci)
                for kz in range(1, outer):
                    copy(every.at[slot], slot, along + kz - 1, place(kz, qi, ci)).start()
            for plane in across:
                slot = place(0, plane, ci)
                copy(every.at[slot], slot, core, place(0, qi, 1 - ci)).start()

        def third():
            for kz in range(1, outer):
                copy(*several(inner), along + kz - 1, place(kz, qi, ci)).wait_recv()
                for plane in (qi,) + across:
                    slot = place(-kz, plane, ci)
                    copy(every.at[slot], slot, core, place(0, qi, 1 - ci)).start()

        def last():
            copy(*several(n // 2), core, place(0, qi, 1 - ci)).wait_recv()

        def drain():
            copy(*several(n - 1), core, place(0, qi, 1 - ci)).wait_send()

        return first, second, third, last, drain

    res_first, res_second, res_third, res_last, res_drain = plane_gather(res_own, res_all, res_send, res_recv)
    norm_first()
    enc_first()
    res_first()
    norm_second()
    enc_second((1,))
    res_second()
    enc_second((2,3))
    norm_third()
    norm_fourth()
    norm_last()
    loads[0].wait()
    scatter(project(wq), q_out, q_in, q_send, q_recv)
    enc_third()
    enc_fourth()
    enc_last()

    tok_rows = enc_own.shape[0]
    group = 32 // tok_rows

    def unpack(j, carry):
        block = enc_all[pl.ds(j * group, group), :, wide_a:3 * wide_a].astype(jnp.float32)
        enc_rows[pl.ds(pl.multiple_of(j * 32, 32), 32), :] = block.reshape(32, -1).astype(jnp.bfloat16)
        return carry

    lax.fori_loop(0, n // group, unpack, 0)
    each_tile = TILE_LEN // tok_rows

    def own_tile(every, cols):
        rows = None
        for t in range(n // each_tile):
            there = every[t * each_tile:(t + 1) * each_tile, :, cols].astype(jnp.float32)
            there = there.reshape(TILE_LEN, -1)
            if rows is None:
                rows, chosen = there, jnp.broadcast_to(tile_own[0], there.shape)
            else:
                rows = jnp.where(chosen == t, there, rows)
        return rows

    queries = own_tile(enc_all, slice(0, wide_a)).astype(jnp.bfloat16)
    columns = [None] * (wide_a // HD)
    scored = []
    for h in range(EH):
        low, high = h * EHD // HD, (h * EHD + EHD - 1) // HD + 1
        span = slice(low * HD, high * HD)
        lane = lax.broadcasted_iota(jnp.int32, (1, (high - low) * HD), 1) + low * HD
        inside = (lane >= h * EHD) & (lane < (h + 1) * EHD)
        picked = jnp.where(inside, queries[:, span], jnp.zeros((), jnp.bfloat16))
        scores = lax.dot_general(
            picked, enc_rows[:, span], (((1,), (1,)), ((), ())), preferred_element_type=jnp.float32
        )
        scored.append((low, high, inside, scores))
    for low, high, inside, scores in scored:
        powers = jnp.exp2((scores - jnp.max(scores, axis=-1, keepdims=True)) * (EHD ** (-0.5) * LOG2E))
        weights = (powers * (1.0 / jnp.sum(powers, axis=-1, keepdims=True))).astype(jnp.bfloat16)
        part = jnp.dot(
            weights, enc_rows[:, wide_a + low * HD:wide_a + high * HD], preferred_element_type=jnp.float32
        )
        for b in range(low, high):
            here = slice((b - low) * HD, (b - low + 1) * HD)
            columns[b] = part[:, here] if columns[b] is None else jnp.where(inside[:, here], part[:, here], columns[b])
    enc_attn = jnp.concatenate(columns, axis=1).astype(jnp.bfloat16)
    loads[1].wait()
    mixed_ref[...] = jnp.dot(enc_attn, weo[...], preferred_element_type=jnp.float32)
    res_third()
    loads[3].wait()
    collect(q_out, q_in, q_send, q_recv)
    width = new_kv.shape[1] // 2
    kv_heads = width // HD
    each = heads // kv_heads
    flip = (((1,), (1,)), ((), ()))
    scale = HD ** (-0.5) * LOG2E
    query = head_rows[...].astype(jnp.bfloat16)
    old = jnp.concatenate(
        [
            lax.dot_general(
                query[g * each:(g + 1) * each, :], cache[:, :, g * HD:(g + 1) * HD].reshape(-1, HD),
                flip, preferred_element_type=jnp.float32,
            )
            for g in range(kv_heads)
        ],
        axis=0,
    ) * scale
    token = lax.broadcasted_iota(jnp.int32, old.shape, 1)
    cached = token // TILE_LEN < jnp.broadcast_to(count_own[0], token.shape)
    old = jnp.where(cached, old, -jnp.inf)
    old_top = jnp.max(old, axis=-1, keepdims=True)
    old = jnp.where(cached, jnp.exp2(old - old_top), 0.0)
    old_total = jnp.sum(old, axis=-1, keepdims=True)
    old = old.astype(jnp.bfloat16)
    old_attn = jnp.concatenate(
        [
            jnp.dot(
                old[g * each:(g + 1) * each, :], cache[:, :, width + g * HD:width + (g + 1) * HD].reshape(-1, HD),
                preferred_element_type=jnp.float32,
            )
            for g in range(kv_heads)
        ],
        axis=0,
    )
    res_last()
    resid = own_tile(res_all, slice(0, res_own.shape[1])) + mixed_ref[...]
    features = layer_norm(resid).astype(jnp.bfloat16)

    loads[2].wait()
    new_kv[:, :width] = jnp.dot(features, wkv[:, :width], preferred_element_type=jnp.float32).astype(jnp.bfloat16)
    new = jnp.concatenate(
        [
            lax.dot_general(
                query[g * each:(g + 1) * each, :], new_kv[:, g * HD:(g + 1) * HD],
                flip, preferred_element_type=jnp.float32,
            )
            for g in range(kv_heads)
        ],
        axis=0,
    ) * scale
    top = jnp.maximum(old_top, jnp.max(new, axis=-1, keepdims=True))
    new = jnp.exp2(new - top)
    keep = jnp.exp2(old_top - top)
    share = 1.0 / (jnp.sum(new, axis=-1, keepdims=True) + old_total * keep)
    new = (new * share).astype(jnp.bfloat16)
    new_kv[:, width:] = jnp.dot(features, wkv[:, width:], preferred_element_type=jnp.float32).astype(jnp.bfloat16)
    new_attn = jnp.concatenate(
        [
            jnp.dot(
                new[g * each:(g + 1) * each, :], new_kv[:, width + g * HD:width + (g + 1) * HD],
                preferred_element_type=jnp.float32,
            )
            for g in range(kv_heads)
        ],
        axis=0,
    )
    dec_attn = (old_attn * (keep * share) + new_attn).astype(jnp.bfloat16)
    norm_drain()
    attn_own[...] = dec_attn
    attn_all[me] = dec_attn
    widen(attn_all, me)
    attn_first, attn_second, attn_third, attn_fourth, attn_last, attn_drain = gather(
        attn_own, attn_all, norm_send, norm_recv, False, widen
    )
    attn_first()
    attn_second()
    attn_third()
    attn_fourth()
    attn_last()
    loads[4].wait()
    scatter(project(wo), o_out, o_in, q_send, q_recv)
    enc_drain()
    res_drain()
    attn_drain()
    collect(o_out, o_in, q_send, q_recv)
    result = (x_rows[...] + head_rows[...]).astype(jnp.bfloat16)
    out_ref[...] = result.reshape(1, -1)


def fused(n, enc_x, enc_qkv, w_eo, w_kv, dec_x, w_q, w_o, cache_kv, doc_tile, cached_count):
    tok_rows = enc_x.shape[0]
    packed = (tok_rows, enc_qkv.shape[1] * enc_qkv.shape[2])
    heads = dec_x.shape[1] // HD
    tokens = n * tok_rows
    bf16, f32 = jnp.bfloat16, jnp.float32
    vmem = pl.BlockSpec(memory_space=pltpu.VMEM)
    hbm = pl.BlockSpec(memory_space=pl.ANY)
    dma = pltpu.SemaphoreType.DMA
    marks = n // 2
    piece = [pltpu.VMEM((heads, HD), bf16), pltpu.VMEM((n, heads, HD), bf16), dma((1,)), dma((marks,))]
    trade = [pltpu.VMEM((n, 2, HD), f32), pltpu.VMEM((2 * n, HD), f32), dma((1,)), dma((1,))]
    return pl.pallas_call(
        functools.partial(fused_kernel, n),
        out_shape=pltpu.VMEM(dec_x.shape, bf16),
        in_specs=[hbm] * 10,
        out_specs=vmem,
        scratch_shapes=[
            pltpu.VMEM(w_eo.shape, bf16),
            pltpu.VMEM(w_kv.shape, bf16),
            pltpu.VMEM(w_q.shape, bf16),
            pltpu.VMEM(w_o.shape, bf16),
            pltpu.VMEM(cache_kv.shape[1:], bf16),
            dma((12,)),
            pltpu.VMEM(dec_x.shape, bf16),
            pltpu.SMEM((1,), jnp.int32),
            pltpu.SMEM((1,), jnp.int32),
            pltpu.VMEM(packed, bf16),
            pltpu.VMEM((n,) + packed, bf16),
            dma((1,)),
            dma((7,)),
            pltpu.VMEM(enc_x.shape, bf16),
            pltpu.VMEM((n,) + enc_x.shape, bf16),
            dma((1,)),
            dma((7,)),
            pltpu.VMEM((TILE_LEN, enc_x.shape[1]), f32),
            pltpu.VMEM((tokens, 2 * enc_qkv.shape[2]), bf16),
            pltpu.VMEM((TILE_LEN, w_kv.shape[1]), bf16),
            pltpu.VMEM((heads, HD), f32),
            *piece,
            *piece[:2],
            pltpu.VMEM((n * (heads + 8), HD), f32),
            pltpu.VMEM((heads, HD), f32),
            *trade,
            *trade[:2],
        ],
        compiler_params=pltpu.CompilerParams(collective_id=0, has_side_effects=True),
    )(enc_qkv.transpose(1, 0, 2), enc_x, dec_x, doc_tile, cached_count, w_eo, w_kv, w_q, w_o, cache_kv[0])

def solution(mesh):
    n = mesh.shape["seq"]
    return jax.shard_map(
        functools.partial(fused, n) if n == 32 else local,
        mesh=mesh,
        in_specs=(
            P(("group", "seq"), None),
            P(("group", "seq"), None, None),
            P(),
            P(),
            P(("group", "seq"), None),
            P(None, "seq"),
            P(None, "seq"),
            P(("group", "seq"), None, None, None),
            P(("group", "seq")),
            P(("group", "seq")),
        ),
        out_specs=P(("group", "seq"), None),
        check_vma=False,
    )
```
